32 devices in a mesh: cells: 8 (over y, x, core), grp: 4 (over z).
Axes of the slice: x: 2, y: 2, z: 4, core: 2. Of those that a mesh axis runs over, the one named last changes fastest.
Arguments:
- fraction: float32 [3, 8, 4, 512], P(None, 'cells', 'grp'), may hold values from 0 to 1
- velocity: float32 [3, 8, 4, 512], P(None, 'cells', 'grp'), may hold values from -1.8 to 1.8
- anchor: int32 [3, 8, 4, 512], P(None, 'cells', 'grp'), may hold values from 0 to 254, as said below
- atom_types: int32 [8, 4, 512], P('cells', 'grp'), may hold values from 0 to 7
- counts: int32 [8, 4], P('cells', 'grp'), may hold values from 64 to 512, as said below
- type_table: float32 [3, 8], replicated, may hold values from 0.7 to 2.8, as said below
- target: float32 [32, 64, 256], P('cells', 'grp'), may hold values from -0.3 to 0.3
Outputs:
- final_velocity: float32 [3, 8, 4, 512], P(None, 'cells', 'grp')
- displacement: float32 [3, 8, 4, 512], P(None, 'cells', 'grp')
- potential: float32 [32, 64, 256], P('cells', 'grp')
The draws below stay inside these ranges and needn't reach their ends.
Inputs may be any that keep to these rules, and one draw needn't show every extreme that they name: `counts`: some cell holds exactly 512 live atoms in every draw; dead slots follow the live ones. `anchor`: component 0 is below 4, component 1 below 16, component 2 below 255. `type_table`: all entries are positive.
All inputs are finite; a program needn't handle non-finite values.
Results may differ from the reference program's by a relative error of at most 0.0003.
Values sent between devices are 32-bit elements; how exact they have to be, the bound alone decides.
A program may use at most 64 MiB of HBM per device.

```python
import jax
import jax.numpy as jnp
from jax import lax

BX = 4
BYD = 16
GZ = 256
ATOM_DEV = 512
TYPES = 8
STEPS = 2
NX = 32
NY = 64
N_CELLS = 8
N_GRP = 4


def draw_counts(key, part):
    first_key, second_key = jax.random.split(jax.random.fold_in(key, 11))
    levels = jax.random.randint(first_key, (N_CELLS, N_GRP), 0, 4, dtype=jnp.int32)
    values = (ATOM_DEV // jnp.power(jnp.int32(2), levels)).astype(jnp.int32)
    chosen = jax.random.randint(second_key, (), 0, N_CELLS * N_GRP, dtype=jnp.int32)
    values = values.reshape(-1).at[chosen].set(ATOM_DEV).reshape(N_CELLS, N_GRP)
    return values.astype(jnp.int32)


def draw_anchor(key, part):
    base_key = jax.random.fold_in(key, 23)
    raw_key, band_key, phase_key, pick_key, spare_key, chosen_key = jax.random.split(base_key, 6)
    raw_values = jax.random.randint(raw_key, (3, N_CELLS, N_GRP, ATOM_DEV), 0, 1048576, dtype=jnp.int32)
    band_width = min(24, GZ // 2)
    swing_depth = min(16, GZ - 1 - band_width)
    band_base = jax.random.randint(band_key, (), 0, GZ - band_width - swing_depth, dtype=jnp.int32)
    phase_shift = jax.random.randint(phase_key, (), 0, 2 * swing_depth, dtype=jnp.int32)
    cell_rows = jnp.arange(N_CELLS, dtype=jnp.int32)[:, None]
    cell_columns = jnp.arange(N_GRP, dtype=jnp.int32)[None, :]
    triangle = jnp.abs((cell_rows + cell_columns + phase_shift) % (2 * swing_depth) - swing_depth)
    in_band = band_base + triangle[:, :, None] + raw_values[2] % band_width
    background = jax.random.randint(spare_key, (N_CELLS, N_GRP, ATOM_DEV), 0, GZ - 1, dtype=jnp.int32)
    picked = jax.random.randint(pick_key, (N_CELLS, N_GRP, ATOM_DEV), 0, 8, dtype=jnp.int32) == 0
    depth_values = jnp.where(picked, background, in_band)
    chosen = jax.random.randint(chosen_key, (), 0, N_CELLS * N_GRP, dtype=jnp.int32)
    depth_values = depth_values.reshape(N_CELLS * N_GRP, ATOM_DEV).at[chosen, 0].set(GZ - 2).reshape(N_CELLS, N_GRP, ATOM_DEV)
    first_values = raw_values[0] % BX
    second_values = raw_values[1] % BYD
    return jnp.stack([first_values, second_values, depth_values]).astype(jnp.int32)


def draw_type_table(key, part):
    amp_key, width_key, mass_key = jax.random.split(jax.random.fold_in(key, 37), 3)
    amplitude = jnp.exp(jax.random.uniform(amp_key, (TYPES,), jnp.float32, jnp.log(0.7), jnp.log(2.0)))
    widths = jax.random.uniform(width_key, (TYPES,), jnp.float32, 1.7, 2.4)
    masses = jnp.exp(jax.random.uniform(mass_key, (TYPES,), jnp.float32, jnp.log(0.7), jnp.log(2.0)))
    return jnp.stack([amplitude, widths, masses]).astype(jnp.float32)


def set_ends(values, own_key, low, top_value):
    place = [jax.random.randint(jax.random.fold_in(own_key, axis), (), 0, length) for axis, length in enumerate(values.shape)]
    widest = values.shape.index(max(values.shape))
    neighbour = place[:widest] + [(place[widest] + 1) % values.shape[widest]] + place[widest + 1:]
    return values.at[tuple(place)].set(low).at[tuple(neighbour)].set(top_value)


def steps_of(key, shape, shards, low, high):
    factor_of = 1.0
    for dim, shards_of in shards:
        draws = jax.random.uniform(jax.random.fold_in(jax.random.fold_in(key, 6), dim), (shards_of,), jnp.float32, low / len(shards), high / len(shards))
        factor_of = factor_of * jnp.repeat(jnp.exp(draws), shape[dim] // shards_of).reshape((-1,) + (1,) * (len(shape) - 1 - dim))
    return factor_of


def gaussian(stream_key, dims, deviation, limit, cuts=(), kind=jnp.bfloat16):
    values = deviation * jax.random.normal(stream_key, dims, jnp.float32)
    if cuts:
        values = values * steps_of(stream_key, dims, cuts, -0.22, 0.18)
    return jnp.clip(values, -limit, limit).astype(kind)


def setup_inputs(seed: int = 0) -> dict:
    keys = jax.random.split(jax.random.key(seed), 8)
    return {
        "fraction": jnp.clip(1.0 * jax.random.uniform(keys[0], (3, N_CELLS, N_GRP, ATOM_DEV), jnp.float32) ** steps_of(keys[0], (3, N_CELLS, N_GRP, ATOM_DEV), ((1, 8), (2, 4)), -0.2, 0.2), 0.0, 1.0),
        "velocity": gaussian(keys[1], (3, N_CELLS, N_GRP, ATOM_DEV), 0.3, 1.8, ((1, 8), (2, 4)), jnp.float32),
        "anchor": draw_anchor(jax.random.fold_in(keys[7], 71), 0),
        "atom_types": set_ends(jax.random.randint(keys[3], (N_CELLS, N_GRP, ATOM_DEV), 0, TYPES), jax.random.fold_in(keys[3], 1), 0, TYPES - 1).astype(jnp.int32),
        "counts": draw_counts(jax.random.fold_in(keys[7], 71), 0),
        "type_table": draw_type_table(jax.random.fold_in(keys[7], 71), 0),
        "target": gaussian(keys[6], (NX, NY, GZ), 0.05, 0.3, ((0, 8), (1, 4)), jnp.float32),
    }


EPSILON = 1e-06
TIME_STEP = 0.5
BLUR_KERNEL = (1.0 / 16.0, 4.0 / 16.0, 6.0 / 16.0, 4.0 / 16.0, 1.0 / 16.0)
BOX_KERNEL = (1.0 / 9.0,) * 9

def tap_valid(values, along_axis, kernel):
    radius = (len(kernel) - 1) // 2
    length = values.shape[along_axis] - 2 * radius
    summed = kernel[0] * lax.slice_in_dim(values, 0, length, axis=along_axis)
    for offset in range(1, len(kernel)):
        summed = summed + kernel[offset] * lax.slice_in_dim(values, offset, offset + length, axis=along_axis)
    return summed

def tap_padded(values, along_axis, kernel):
    radius = (len(kernel) - 1) // 2
    widths = [(0, 0)] * values.ndim
    widths[along_axis] = (radius, radius)
    return tap_valid(jnp.pad(values, widths), along_axis, kernel)

def filter_three(values, kernel):
    return tap_padded(tap_padded(tap_padded(values, 0, kernel), 1, kernel), 2, kernel)

def corner_weights(position, fraction, extent):
    places = jnp.arange(extent, dtype=jnp.float32)
    lower = (position[:, None] == places[None, :]).astype(jnp.float32)
    upper = (position[:, None] + 1.0 == places[None, :]).astype(jnp.float32)
    return (lower * (1.0 - fraction[:, None]) + upper * fraction[:, None], upper - lower)

def spread_brick(anchors, fractions, amounts, extent_x, extent_y, extent_z):
    atom_count = anchors.shape[1]
    weight_x = corner_weights(anchors[0], fractions[0], extent_x)[0]
    weight_y = corner_weights(anchors[1], fractions[1], extent_y)[0]
    weight_z = corner_weights(anchors[2], fractions[2], extent_z)[0]
    plane = (weight_x[:, :, None] * weight_y[:, None, :]).reshape(atom_count, extent_x * extent_y)
    depth = weight_z * amounts[:, None]
    summed = lax.dot_general(plane, depth, (((0,), (0,)), ((), ())), precision=lax.Precision.HIGHEST, preferred_element_type=jnp.float32)
    return summed.reshape(extent_x, extent_y, extent_z)

def sample_gradient(anchors, fractions, field):
    extent_x, extent_y, extent_z = field.shape
    atom_count = anchors.shape[1]
    weight_x, slope_x = corner_weights(anchors[0], fractions[0], extent_x)
    weight_y, slope_y = corner_weights(anchors[1], fractions[1], extent_y)
    weight_z, slope_z = corner_weights(anchors[2], fractions[2], extent_z)
    matrix = field.reshape(extent_x * extent_y, extent_z)
    stacked = jnp.concatenate([weight_z, slope_z], 0)
    product = lax.dot_general(stacked, matrix, (((1,), (1,)), ((), ())), precision=lax.Precision.HIGHEST, preferred_element_type=jnp.float32)
    product = product.reshape(2, atom_count, extent_x, extent_y)
    grad_x = jnp.einsum('ax,ay,axy->a', slope_x, weight_y, product[0], precision=lax.Precision.HIGHEST)
    grad_y = jnp.einsum('ax,ay,axy->a', weight_x, slope_y, product[0], precision=lax.Precision.HIGHEST)
    grad_z = jnp.einsum('ax,ay,axy->a', weight_x, weight_y, product[1], precision=lax.Precision.HIGHEST)
    return jnp.stack([grad_x, grad_y, grad_z])

def pair_block(own, others):
    offsets = own[0:3, :, None] - others[0:3, None, :] + (own[3:6, :, None] - others[3:6, None, :])
    distance = lax.optimization_barrier(jnp.sum(offsets * offsets, 0))
    spread = own[7][:, None] + others[7][None, :]
    coupling = others[6][None, :] * jnp.exp(-0.5 * distance / spread) / spread
    return own[6][None, :] * lax.optimization_barrier(jnp.sum(coupling[None] * offsets, 2))

def type_values(kinds, table):
    matches = (kinds[..., None] == jnp.arange(table.shape[1], dtype=jnp.int32)).astype(jnp.float32)
    shaped = table.reshape((3,) + (1,) * kinds.ndim + (table.shape[1],))
    return lax.optimization_barrier(jnp.sum(matches[None] * shaped, -1))

def cell_pairs(own, others):
    block_size = min(128, own.shape[1])
    blocks = own.reshape(8, -1, block_size).transpose(1, 0, 2)
    result = lax.map(lambda piece: pair_block(piece, others), blocks)
    return result.transpose(1, 0, 2).reshape(3, -1)

def all_pairs(packet):
    padded = jnp.pad(packet, ((0, 0), (1, 1), (1, 1), (0, 0)))

    def per_slab(slab_index):
        window = lax.dynamic_slice(padded, (jnp.int32(0), slab_index, jnp.int32(0), jnp.int32(0)), (8, 3, N_GRP + 2, ATOM_DEV))
        pieces = []
        for quarter in range(N_GRP):
            others = window[:, :, quarter:quarter + 3, :].reshape(8, 9 * ATOM_DEV)
            pieces.append(cell_pairs(window[:, 1, quarter + 1, :], others))
        return jnp.stack(pieces, 1)
    result = lax.map(per_slab, jnp.arange(N_CELLS, dtype=jnp.int32))
    return result.transpose(1, 0, 2, 3)

def full_density(anchor_local, fraction, charge):

    def per_slab(inputs):
        anchors, fractions, amounts = inputs
        return jnp.stack([spread_brick(anchors[:, quarter], fractions[:, quarter], amounts[quarter], BX + 1, BYD + 1, GZ) for quarter in range(N_GRP)])
    bricks = lax.map(per_slab, (jnp.moveaxis(anchor_local, 1, 0), jnp.moveaxis(fraction, 1, 0), charge))
    rows_out = bricks[:, :, BX]
    arrived = jnp.concatenate([jnp.zeros_like(rows_out[:1]), rows_out[:-1]], 0)
    upper = bricks[:, :, :BX].at[:, :, 0].add(arrived)
    columns = upper[:, :, :, BYD]
    arrived_side = jnp.concatenate([jnp.zeros_like(columns[:, :1]), columns[:, :-1]], 1)
    inner = upper[:, :, :, :BYD].at[:, :, :, 0].add(arrived_side)
    return inner.transpose(0, 2, 1, 3, 4).reshape(NX, NY, GZ)

def full_gradient(anchor_local, fraction, field):
    padded = jnp.pad(field, ((0, 1), (0, 1), (0, 0)))

    def per_slab(inputs):
        slab_index, anchors, fractions = inputs
        planes = lax.dynamic_slice_in_dim(padded, slab_index * BX, BX + 1, 0)
        return jnp.stack([sample_gradient(anchors[:, quarter], fractions[:, quarter], planes[:, quarter * BYD:quarter * BYD + BYD + 1]) for quarter in range(N_GRP)], 1)
    result = lax.map(per_slab, (jnp.arange(N_CELLS, dtype=jnp.int32), jnp.moveaxis(anchor_local, 1, 0), jnp.moveaxis(fraction, 1, 0)))
    return result.transpose(1, 0, 2, 3)

def reference(fraction, velocity, anchor, atom_types, counts, type_table, target):
    live = (jnp.arange(ATOM_DEV, dtype=jnp.int32)[None, None, :] < counts[:, :, None]).astype(jnp.float32)
    properties = type_values(atom_types, type_table)
    charge = properties[0] * live
    square_width = properties[1] * properties[1]
    masses = properties[2]
    first_x = jnp.broadcast_to((jnp.arange(N_CELLS, dtype=jnp.int32) * BX)[:, None], (N_CELLS, N_GRP))
    first_y = jnp.broadcast_to((jnp.arange(N_GRP, dtype=jnp.int32) * BYD)[None, :], (N_CELLS, N_GRP))
    root = jnp.stack([first_x, first_y, jnp.zeros((N_CELLS, N_GRP), jnp.int32)])
    anchor_local = anchor.astype(jnp.float32)
    anchor_global = (anchor + root[..., None]).astype(jnp.float32)
    mean_one = filter_three(target, BOX_KERNEL)
    mean_two = filter_three(target * target, BOX_KERNEL)
    inverse_scale = lax.rsqrt(mean_two - mean_one * mean_one + EPSILON)
    moved = jnp.zeros_like(velocity)
    potential = jnp.zeros_like(target)
    for turn_index in range(STEPS):
        packet = jnp.concatenate([anchor_global, fraction, charge[None], square_width[None]], 0)
        forces = all_pairs(packet)
        density = full_density(anchor_local, fraction, charge)
        residual = (filter_three(density, BLUR_KERNEL) - target) * inverse_scale
        potential = filter_three(residual, BLUR_KERNEL)
        gradient = full_gradient(anchor_local, fraction, potential)
        forces = forces - charge[None] * gradient
        velocity = velocity + TIME_STEP * forces / masses[None]
        moved = moved + TIME_STEP * velocity
        fraction = fraction + TIME_STEP * velocity
    return (velocity * live[None], moved * live[None], potential)
```

```python
import functools
import math

import jax
import jax.numpy as jnp
from jax import lax
from jax.experimental import pallas as pl
from jax.experimental.pallas import tpu as pltpu
from jax.sharding import PartitionSpec as P

EPSILON = 1e-06
TIME_STEP = 0.5
TAPS = (1.0 / 16.0, 4.0 / 16.0, 6.0 / 16.0, 4.0 / 16.0, 1.0 / 16.0)
F32 = jnp.float32
BF16 = jnp.bfloat16
RX, RY = 2, 1
NB = 2 * RY + 1
SLOTS = (2 * RX + 1) * NB
OWN = RX * NB + RY
MESH = pl.DeviceIdType.MESH
VMEM = pl.BlockSpec(memory_space=pltpu.VMEM)
SMEM = pl.BlockSpec(memory_space=pltpu.SMEM)
ANY = pl.BlockSpec(memory_space=pl.ANY)
NEIGHBOURS = tuple(
    (a, b) for a in range(-RX, RX + 1) for b in range(-RY, RY + 1) if (a, b) != (0, 0)
)


def slot_of(a, b):
    return (a + RX) * NB + (b + RY)


def exists(a, b):
    s = lax.axis_index("cells") + a
    q = lax.axis_index("grp") + b
    ns, nq = lax.axis_size("cells"), lax.axis_size("grp")
    return (s >= 0) & (s < ns) & (q >= 0) & (q < nq)


def target_piece(a, b, bx, by):
    x0 = max(0, -6 - a * bx)
    x1 = min(bx, bx + 7 - a * bx)
    y0, y1 = {-1: (by - 8, by), 0: (0, by), 1: (0, 8)}[b]
    return x0, x1, y0, y1


def split2(x):
    hi = x.astype(BF16)
    return hi, (x - hi.astype(F32)).astype(BF16)


def split3(x):
    hi = x.astype(BF16)
    rest = x - hi.astype(F32)
    mid = rest.astype(BF16)
    return hi, mid, (rest - mid.astype(F32)).astype(BF16)


def dot_nn(x, y):
    return lax.dot_general(x, y, (((1,), (0,)), ((), ())), preferred_element_type=F32)


def dot_nt(x, y):
    return lax.dot_general(x, y, (((1,), (1,)), ((), ())), preferred_element_type=F32)


def iota_f(shape, dim):
    return lax.broadcasted_iota(jnp.int32, shape, dim).astype(F32)


def tap_of(t):
    u = jnp.abs(t)
    return jnp.where(
        u == 0.0, TAPS[2], jnp.where(u == 1.0, TAPS[1], jnp.where(u == 2.0, TAPS[0], 0.0))
    )


def band(gz, radius, taps):
    i = lax.broadcasted_iota(jnp.int32, (gz, gz), 0)
    j = lax.broadcasted_iota(jnp.int32, (gz, gz), 1)
    t = (i - j).astype(F32)
    if taps:
        return tap_of(t).astype(BF16)
    return jnp.where(jnp.abs(t) <= radius, 1.0, 0.0).astype(BF16)


def pack(fraction, anchor, kinds, counts, table, packet, mass):
    atoms = packet.shape[1]
    n = counts[0, 0]
    kind = kinds[0]
    lane = lax.broadcasted_iota(jnp.int32, (1, atoms), 1)
    rows = []
    for r in range(3):
        row = jnp.zeros((1, atoms), F32)
        for t in range(table.shape[1]):
            row = jnp.where(kind == t, table[r, t], row)
        rows.append(row)
    packet[0:3] = anchor[:, 0, 0, :].astype(F32)
    packet[3:6] = fraction[:, 0, 0, :]
    packet[6:7] = jnp.where(lane < n, rows[0], 0.0)
    packet[7:8] = rows[1] * rows[1]
    mass[...] = rows[2]


SPREAD = -2.0 / math.log2(math.e)


def kernel(steps, bx, by, gz, n_x, n_y, *refs):
    (fraction, velocity, anchor, kinds, own_counts, table, target,
     vel_out, moved_out, pot,
     packet, mass, packets, wide, now, later, vel, moved,
     pk, pos, feat, hot, cols, acc, tile, other_tile, dens, dens_up, inv_ref, tgt_ref,
     send_sem, recv_sem) = refs
    atoms = packet.shape[1]
    s, q = lax.axis_index("cells"), lax.axis_index("grp")
    rx, ry = bx + 5, by + 8
    others = [(a, b) for a, b in NEIGHBOURS if abs(a) <= 1]
    others = others + [(a, b) for a, b in NEIGHBOURS if abs(a) > 1]

    barrier = pltpu.get_barrier_semaphore()
    total = jnp.int32(0)
    for a, b in NEIGHBOURS:
        there = exists(a, b)
        total = total + there.astype(jnp.int32)

        @pl.when(there)
        def _(a=a, b=b):
            pl.semaphore_signal(barrier, inc=1, device_id=(s + a, q + b), device_id_type=MESH)

    pack(fraction, anchor, kinds, own_counts, table, packet, mass)
    vel[...] = velocity[:, 0, 0, :]
    moved[...] = jnp.zeros_like(moved)
    pl.semaphore_wait(barrier, total)

    def packet_copy(src, dst, group, a, b, there):
        mine, back = slot_of(a, b), slot_of(-a, -b)
        slot = back if there else mine
        return pltpu.make_async_remote_copy(
            src_ref=src,
            dst_ref=dst.at[slot],
            send_sem=send_sem.at[group, mine],
            recv_sem=recv_sem.at[group, slot],
            device_id=(s + a, q + b),
            device_id_type=MESH,
        )

    def target_copy(a, b, there):
        mine, back = slot_of(a, b), slot_of(-a, -b)
        slot = back if there else mine
        c, d = (-a, -b) if there else (a, b)
        x0, x1, y0, y1 = target_piece(c, d, bx, by)
        X, Y = 6 + c * bx + x0, 8 + d * by + y0
        return pltpu.make_async_remote_copy(
            src_ref=target.at[x0:x1, y0:y1],
            dst_ref=wide.at[X : X + x1 - x0, Y : Y + y1 - y0],
            send_sem=send_sem.at[1, mine],
            recv_sem=recv_sem.at[1, slot],
            device_id=(s + a, q + b),
            device_id_type=MESH,
        )

    def each(cells, act):
        for a, b in cells:

            @pl.when(exists(a, b))
            def _(a=a, b=b):
                act(a, b)

    each(others, lambda a, b: packet_copy(packet, packets, 0, a, b, True).start())
    each(others, lambda a, b: target_copy(a, b, True).start())

    row = lax.broadcasted_iota(jnp.int32, (8, atoms), 0)
    iz = iota_f((gz, atoms), 0).astype(BF16)

    def load_cell(step, a, b):
        slot = slot_of(a, b)
        own = slot == OWN
        if step == 0:
            block = packet[...] if own else packets[slot]
            if not own:
                block = jnp.where(exists(a, b), block, 0.0)
            hot[slot] = jnp.where(
                iz == block[2:3].astype(BF16), jnp.ones((), BF16), jnp.zeros((), BF16)
            )
        else:
            block = pk[slot]
            fresh = now[...] if own else jnp.where(exists(a, b), later[slot], 0.0)
            block = jnp.concatenate([block[0:3], fresh, block[6:8]], 0)
        pk[slot] = block
        if abs(a) <= 1:
            base = jnp.where(row == 0, float(a * bx), jnp.where(row == 1, float(b * by), 0.0))
            place = jnp.where(
                row < 3, block + pltpu.roll(block, 5, 0) + base, pltpu.roll(block, 4, 0) * SPREAD
            )
            pos[slot] = place
            four = jnp.where(row < 3, place, jnp.where(row == 3, 1.0, 0.0)) * block[6:7]
            h, m, l = split3(four)
            feat[slot] = jnp.concatenate(
                [h.astype(F32), m.astype(F32), l.astype(F32), jnp.zeros_like(four)], 0
            )

    def multiply():
        acc[...] += dot_nt(tile[...], other_tile[...])

    def pair_slot(slot):
        multiply()
        for k in range(0, atoms, 128):
            at = slice(k, k + 128)
            other = pos[slot, :, at]
            dx = cols[0] - other[0:1]
            dy = cols[1] - other[1:2]
            dz = cols[2] - other[2:3]
            d2 = dx * dx + dy * dy + dz * dz
            inverse = 1.0 / (cols[3] + other[3:4])
            value = jnp.exp2(d2 * inverse) * inverse
            hi, lo = split2(value)
            tile[:, 2 * k : 2 * k + 128] = hi
            tile[:, 2 * k + 128 : 2 * k + 256] = lo
            f = feat[slot, :, at].astype(BF16)
            other_tile[:, 2 * k : 2 * k + 128] = f
            other_tile[:, 2 * k + 128 : 2 * k + 256] = f

    def spread(a, b):
        p0 = max(0, a * bx)
        p1 = min(rx, a * bx + bx + 5)
        r0, r1 = {-1: (0, 8), 0: (0, ry), 1: (by, ry)}[b]
        slot = slot_of(a, b)
        block = pk[slot]
        charge = block[6:7]
        ax, ay = block[0:1], block[1:2]
        fx, fy, fz = block[3:4], block[4:5], block[5:6]
        ax = ax + float(a * bx)
        ay = ay + float(b * by)
        in_x = ax + 1.0 + (s * bx).astype(F32) < float(n_x)
        in_y = ay + 1.0 + (q * by).astype(F32) < float(n_y)
        ux = jnp.where(in_x, fx, 0.0)
        uy = jnp.where(in_y, fy, 0.0)
        tx = iota_f((p1 - p0, atoms), 0) + float(p0 - 2) - ax
        wx = tap_of(tx) * (1.0 - fx) + tap_of(tx - 1.0) * ux
        ty = iota_f((r1 - r0, atoms), 0) + float(r0 - 2) - ay
        wy = tap_of(ty) * (1.0 - fy) + tap_of(ty - 1.0) * uy
        low, up = charge * (1.0 - fz), charge * fz
        planes = []
        for w in (wx * low, wx * up):
            plane = jnp.concatenate([wy * w[p : p + 1] for p in range(p1 - p0)], 0)
            planes.extend(split2(plane))
        size = planes[0].shape[0]
        out = dot_nt(jnp.concatenate(planes, 0), hot[slot])
        shape = (p1 - p0, r1 - r0, gz)
        dens[p0:p1, r0:r1] += (out[:size] + out[size : 2 * size]).reshape(shape)
        dens_up[p0:p1, r0:r1] += (out[2 * size : 3 * size] + out[3 * size :]).reshape(shape)

    i = lax.broadcasted_iota(jnp.int32, (gz, gz), 0)
    j = lax.broadcasted_iota(jnp.int32, (gz, gz), 1)
    blur_z = tap_of((i - j).astype(F32)).astype(BF16)
    blur_up = tap_of((i + 1 - j).astype(F32)).astype(BF16)

    def z_blur(x, matrix):
        h, l = split2(x)
        size = x.shape[0]
        both = dot_nn(jnp.concatenate([h, l], 0), matrix)
        return both[:size] + both[size:]

    gx = lax.broadcasted_iota(jnp.int32, (rx, ry, gz), 0) - 2 + s * bx
    gy = lax.broadcasted_iota(jnp.int32, (rx, ry, gz), 1) - 2 + q * by
    inside = (gx >= 0) & (gx < n_x) & (gy >= 0) & (gy < n_y)

    def scales():
        wxp, wyp = bx + 13, by + 16
        tx = lax.broadcasted_iota(jnp.int32, (wxp, wyp, gz), 0) - 6 + s * bx
        ty = lax.broadcasted_iota(jnp.int32, (wxp, wyp, gz), 1) - 8 + q * by
        valid = (tx >= 0) & (tx < n_x) & (ty >= 0) & (ty < n_y)
        wide[6 : 6 + bx, 8 : 8 + by] = target[...]
        t = jnp.where(valid, wide[...], 0.0)
        box_z = band(gz, 4, False)

        def boxed(v):
            two = v[:-1] + v[1:]
            four = two[:-2] + two[2:]
            eight = four[:-4] + four[4:]
            v = eight[:rx] + v[8 : 8 + rx]
            size = wyp
            two = v + pltpu.roll(v, size - 1, 1)
            four = two + pltpu.roll(two, size - 2, 1)
            eight = four + pltpu.roll(four, size - 4, 1)
            nine = eight + pltpu.roll(v, size - 8, 1)
            v = pltpu.roll(nine, size - 2, 1)[:, :ry]
            v = v.reshape(rx * ry, gz)
            h, m, l = split3(v)
            size = v.shape[0]
            out = dot_nn(jnp.concatenate([h, m, l], 0), box_z)
            out = out[:size] + out[size : 2 * size] + out[2 * size :]
            return out.reshape(rx, ry, gz) * (1.0 / 729.0)

        mean_one = boxed(t)
        mean_two = boxed(t * t)
        inverse_scale = lax.rsqrt(mean_two - mean_one * mean_one + EPSILON)
        inv_ref[...] = jnp.where(inside, inverse_scale, 0.0)
        tgt_ref[...] = pltpu.roll(t[4 : 4 + rx], wyp - 6, 1)[:, :ry]

    def map_part():
        size = rx * ry
        blurred = z_blur(dens[...].reshape(size, gz), blur_z)
        blurred = blurred + z_blur(dens_up[...].reshape(size, gz), blur_up)
        blurred = blurred.reshape(rx, ry, gz)
        residual = jnp.where(inside, (blurred - tgt_ref[...]) * inv_ref[...], 0.0)
        along = TAPS[0] * (residual[0 : bx + 1] + residual[4 : bx + 5])
        along = along + TAPS[1] * (residual[1 : bx + 2] + residual[3 : bx + 4])
        along = along + TAPS[2] * residual[2 : bx + 3]
        down = TAPS[0] * along
        for k in range(1, 5):
            down = down + TAPS[k] * pltpu.roll(along, ry - k, 1)
        return z_blur(down.reshape((bx + 1) * ry, gz), blur_z).reshape(bx + 1, ry, gz)

    def gradient_of(potential):
        px = lax.broadcasted_iota(jnp.int32, (bx + 1, ry, gz), 0) + s * bx
        py = lax.broadcasted_iota(jnp.int32, (bx + 1, ry, gz), 1) + q * by
        py_local = lax.broadcasted_iota(jnp.int32, (bx + 1, ry, gz), 1)
        field = jnp.where((px < n_x) & (py < n_y) & (py_local <= by), potential, 0.0)
        own = pk[OWN]
        ax, ay = own[0:1], own[1:2]
        fx, fy, fz = own[3:4], own[4:5], own[5:6]
        size = (bx + 1) * ry
        field = field.reshape(size, gz)
        up = pltpu.roll(field, gz - 1, 1)
        out = dot_nn(jnp.concatenate(split2(field) + split2(up), 0), hot[OWN])
        at_low = out[:size] + out[size : 2 * size]
        slope = out[2 * size : 3 * size] + out[3 * size :] - at_low
        value = at_low + fz * slope
        iy = iota_f((ry, atoms), 0)
        low_y = jnp.where(iy == ay, 1.0, 0.0)
        up_y = jnp.where(iy == ay + 1.0, 1.0, 0.0)
        wy = low_y * (1.0 - fy) + up_y * fy
        sy = up_y - low_y
        grad_x = jnp.zeros((1, atoms), F32)
        grad_y = jnp.zeros((1, atoms), F32)
        grad_z = jnp.zeros((1, atoms), F32)
        for p in range(bx + 1):
            low_x = jnp.where(ax == float(p), 1.0, 0.0)
            up_x = jnp.where(ax + 1.0 == float(p), 1.0, 0.0)
            wx = low_x * (1.0 - fx) + up_x * fx
            sx = up_x - low_x
            v = value[p * ry : (p + 1) * ry]
            g = slope[p * ry : (p + 1) * ry]
            grad_x = grad_x + sx * jnp.sum(wy * v, 0, keepdims=True)
            grad_y = grad_y + wx * jnp.sum(sy * v, 0, keepdims=True)
            grad_z = grad_z + wx * jnp.sum(wy * g, 0, keepdims=True)
        return own[6:7] * jnp.concatenate([grad_x, grad_y, grad_z], 0)

    for step in range(steps):
        last = step == steps - 1
        group = 0 if step == 0 else step + 1
        source, landing = (packet, packets) if step == 0 else (now, later)
        load_cell(step, 0, 0)
        own_t = jnp.transpose(pos[OWN])
        for k in range(4):
            cols[k] = jnp.broadcast_to(own_t[:, k : k + 1], (atoms, 128))
        acc[...] = jnp.zeros_like(acc)
        tile[...] = jnp.zeros_like(tile)
        other_tile[...] = jnp.zeros_like(other_tile)
        dens[...] = jnp.zeros_like(dens)
        dens_up[...] = jnp.zeros_like(dens_up)
        pair_slot(OWN)
        spread(0, 0)
        each(others, lambda a, b: packet_copy(source, landing, group, a, b, False).wait_recv())
        for a, b in others:
            load_cell(step, a, b)

        def per_slot(k, carry):
            slot = k + NB * (RX - 1)
            pair_slot(slot + (slot >= OWN).astype(jnp.int32))
            return carry

        lax.fori_loop(0, 3 * NB - 1, per_slot, 0)
        multiply()
        for a, b in others:
            spread(a, b)
        if step == 0:
            each(others, lambda a, b: target_copy(a, b, False).wait_recv())
            scales()
        potential = map_part()
        if last:
            pot[...] = potential[:bx, :by]
        gradient = gradient_of(potential)
        sums = jnp.transpose(acc[...])
        sums = sums[0:8] + sums[8:16] + sums[16:24]
        here = pos[OWN][0:3]
        pair = (SPREAD * pk[OWN][6:7]) * (here * sums[3:4] - sums[0:3])
        new_velocity = vel[...] + TIME_STEP * (pair - gradient) / mass[...]
        new_moved = moved[...] + TIME_STEP * new_velocity
        if last:
            live = lax.broadcasted_iota(jnp.int32, (3, atoms), 1) < own_counts[0, 0]
            vel_out[:, 0, 0, :] = jnp.where(live, new_velocity, 0.0)
            moved_out[:, 0, 0, :] = jnp.where(live, new_moved, 0.0)
        else:
            vel[...] = new_velocity
            moved[...] = new_moved
            now[...] = pk[OWN][3:6] + TIME_STEP * new_velocity
            each(others, lambda a, b: packet_copy(now, later, step + 2, a, b, True).start())

    each(others, lambda a, b: packet_copy(packet, packets, 0, a, b, True).wait_send())
    each(others, lambda a, b: target_copy(a, b, True).wait_send())
    for step in range(1, steps):
        each(others, lambda a, b: packet_copy(now, later, step + 1, a, b, True).wait_send())


STEPS = 2


def per_device(fraction, velocity, anchor, atom_types, counts, type_table, target):
    atoms = fraction.shape[3]
    bx, by, gz = target.shape
    n_x = bx * lax.axis_size("cells")
    n_y = by * lax.axis_size("grp")
    final = jax.ShapeDtypeStruct(velocity.shape, F32)
    field = jax.ShapeDtypeStruct((bx, by, gz), F32)
    region = pltpu.VMEM((bx + 5, by + 8, gz), F32)
    three = pltpu.VMEM((3, atoms), F32)
    return tuple(
        pl.pallas_call(
            functools.partial(kernel, STEPS, bx, by, gz, n_x, n_y),
            out_shape=[final, final, field],
            in_specs=[VMEM, VMEM, VMEM, VMEM, SMEM, SMEM, VMEM],
            out_specs=[VMEM] * 3,
            scratch_shapes=[
                pltpu.VMEM((8, atoms), F32),
                pltpu.VMEM((1, atoms), F32),
                pltpu.VMEM((SLOTS, 8, atoms), F32),
                pltpu.VMEM((bx + 13, by + 16, gz), F32),
                three,
                pltpu.VMEM((SLOTS, 3, atoms), F32),
                three,
                three,
                pltpu.VMEM((SLOTS, 8, atoms), F32),
                pltpu.VMEM((SLOTS, 8, atoms), F32),
                pltpu.VMEM((SLOTS, 32, atoms), F32),
                pltpu.VMEM((SLOTS, gz, atoms), BF16),
                pltpu.VMEM((4, atoms, 128), F32),
                pltpu.VMEM((atoms, 32), F32),
                pltpu.VMEM((atoms, 2 * atoms), BF16),
                pltpu.VMEM((32, 2 * atoms), BF16),
                region,
                region,
                region,
                region,
                pltpu.SemaphoreType.DMA((STEPS + 1, SLOTS)),
                pltpu.SemaphoreType.DMA((STEPS + 1, SLOTS)),
            ],
            compiler_params=pltpu.CompilerParams(
                collective_id=0, has_side_effects=True, vmem_limit_bytes=40 * 2**20
            ),
            name="dynamics",
        )(fraction, velocity, anchor, atom_types, counts, type_table, target)
    )


def solution(mesh):
    placed = (
        P(None, "cells", "grp", None),
        P(None, "cells", "grp", None),
        P(None, "cells", "grp", None),
        P("cells", "grp", None),
        P("cells", "grp"),
        P(),
        P("cells", "grp", None),
    )
    return jax.shard_map(
        per_device,
        mesh=mesh,
        in_specs=placed,
        out_specs=(
            P(None, "cells", "grp", None),
            P(None, "cells", "grp", None),
            P("cells", "grp", None),
        ),
        check_vma=False,
    )
```

```python
import functools
import math

import jax
import jax.numpy as jnp
from jax import lax
from jax.experimental import pallas as pl
from jax.experimental.pallas import tpu as pltpu
from jax.sharding import PartitionSpec as P

EPSILON = 1e-06
TIME_STEP = 0.5
TAPS = (1.0 / 16.0, 4.0 / 16.0, 6.0 / 16.0, 4.0 / 16.0, 1.0 / 16.0)
F32 = jnp.float32
BF16 = jnp.bfloat16
RX, RY = 2, 1
NB = 2 * RY + 1
SLOTS = (2 * RX + 1) * NB
OWN = RX * NB + RY
MESH = pl.DeviceIdType.MESH
VMEM = pl.BlockSpec(memory_space=pltpu.VMEM)
SMEM = pl.BlockSpec(memory_space=pltpu.SMEM)
HBM = pl.BlockSpec(memory_space=pltpu.HBM)
NEIGHBOURS = tuple(
    (a, b) for a in range(-RX, RX + 1) for b in range(-RY, RY + 1) if (a, b) != (0, 0)
)


def slot_of(a, b):
    return (a + RX) * NB + (b + RY)


def exists(a, b):
    s = lax.axis_index("cells") + a
    q = lax.axis_index("grp") + b
    ns, nq = lax.axis_size("cells"), lax.axis_size("grp")
    return (s >= 0) & (s < ns) & (q >= 0) & (q < nq)


def target_piece(a, b, bx, by):
    x0 = max(0, -6 - a * bx)
    x1 = min(bx, bx + 7 - a * bx)
    y0, y1 = {-1: (by - 8, by), 0: (0, by), 1: (0, 8)}[b]
    return x0, x1, y0, y1


def split2(x):
    hi = x.astype(BF16)
    return hi, (x - hi.astype(F32)).astype(BF16)


def split3(x):
    hi = x.astype(BF16)
    rest = x - hi.astype(F32)
    mid = rest.astype(BF16)
    return hi, mid, (rest - mid.astype(F32)).astype(BF16)


def dot_nn(x, y):
    return lax.dot_general(x, y, (((1,), (0,)), ((), ())), preferred_element_type=F32)


def dot_nt(x, y):
    return lax.dot_general(x, y, (((1,), (1,)), ((), ())), preferred_element_type=F32)


def iota_f(shape, dim):
    return lax.broadcasted_iota(jnp.int32, shape, dim).astype(F32)


def tap_of(t):
    u = jnp.abs(t)
    return jnp.where(
        u == 0.0, TAPS[2], jnp.where(u == 1.0, TAPS[1], jnp.where(u == 2.0, TAPS[0], 0.0))
    )


def band(gz, radius, taps):
    i = lax.broadcasted_iota(jnp.int32, (gz, gz), 0)
    j = lax.broadcasted_iota(jnp.int32, (gz, gz), 1)
    t = (i - j).astype(F32)
    if taps:
        return tap_of(t).astype(BF16)
    return jnp.where(jnp.abs(t) <= radius, 1.0, 0.0).astype(BF16)


def pack(fraction, anchor, kinds, counts, table, packet, mass):
    atoms = packet.shape[1]
    n = counts[0, 0]
    kind = kinds[0]
    lane = lax.broadcasted_iota(jnp.int32, (1, atoms), 1)
    rows = []
    for r in range(3):
        row = jnp.zeros((1, atoms), F32)
        for t in range(table.shape[1]):
            row = jnp.where(kind == t, table[r, t], row)
        rows.append(row)
    packet[0:3] = anchor[:, 0, 0, :].astype(F32)
    packet[3:6] = fraction[:, 0, 0, :]
    packet[6:7] = jnp.where(lane < n, rows[0], 0.0)
    packet[7:8] = rows[1] * rows[1]
    mass[...] = rows[2]


SPREAD = -2.0 / math.log2(math.e)
FIRST = NB * (RX - 1)


def kernel(steps, bx, by, gz, n_x, n_y, *refs):
    (fraction, velocity, anchor, kinds, own_counts, table_hbm, target,
     vel_out, moved_out, pot,
     fraction_in, velocity_in, anchor_in, kinds_in, table, packet, mass, packets, wide, now, later, vel, moved,
     pk, pos, feat, hot, side_xy, side_type, near_xy, near_type, col_z, xy0, xy1, rates,
     tile0, tile1, acc, dens, dens_up, inv_ref, tgt_ref,
     send_sem, recv_sem, load_sem) = refs
    atoms = packet.shape[1]
    s, q = lax.axis_index("cells"), lax.axis_index("grp")
    rx, ry = bx + 5, by + 8
    near = [(a, b) for a, b in NEIGHBOURS if abs(a) <= 1]
    far = [(a, b) for a, b in NEIGHBOURS if abs(a) > 1]
    others = near + far

    barrier = pltpu.get_barrier_semaphore()
    total = jnp.int32(0)
    for a, b in NEIGHBOURS:
        there = exists(a, b)
        total = total + there.astype(jnp.int32)

        @pl.when(there)
        def _(a=a, b=b):
            pl.semaphore_signal(barrier, inc=1, device_id=(s + a, q + b), device_id_type=MESH)

    own_target = wide.at[6 : 6 + bx, 8 : 8 + by]
    loads = [
        pltpu.make_async_copy(src, dst, load_sem.at[k])
        for k, (src, dst) in enumerate(
            [(anchor, anchor_in), (fraction, fraction_in), (kinds, kinds_in), (table_hbm, table),
             (velocity, velocity_in), (target, own_target)]
        )
    ]
    for load in loads:
        load.start()
    for load in loads[:4]:
        load.wait()
    pack(fraction_in, anchor_in, kinds_in, own_counts, table, packet, mass)
    pl.semaphore_wait(barrier, total)

    def packet_copy(src, dst, group, a, b, there):
        mine, back = slot_of(a, b), slot_of(-a, -b)
        slot = back if there else mine
        return pltpu.make_async_remote_copy(
            src_ref=src,
            dst_ref=dst.at[slot],
            send_sem=send_sem.at[group, mine],
            recv_sem=recv_sem.at[group, slot],
            device_id=(s + a, q + b),
            device_id_type=MESH,
        )

    def target_copy(a, b, there):
        mine, back = slot_of(a, b), slot_of(-a, -b)
        slot = back if there else mine
        c, d = (-a, -b) if there else (a, b)
        x0, x1, y0, y1 = target_piece(c, d, bx, by)
        X, Y = 6 + c * bx + x0, 8 + d * by + y0
        return pltpu.make_async_remote_copy(
            src_ref=target.at[x0:x1, y0:y1],
            dst_ref=wide.at[X : X + x1 - x0, Y : Y + y1 - y0],
            send_sem=send_sem.at[1, mine],
            recv_sem=recv_sem.at[1, slot],
            device_id=(s + a, q + b),
            device_id_type=MESH,
        )

    def each(cells, act):
        for a, b in cells:

            @pl.when(exists(a, b))
            def _(a=a, b=b):
                act(a, b)

    each(others, lambda a, b: packet_copy(packet, packets, 0, a, b, True).start())
    for load in loads[4:]:
        load.wait()
    vel[...] = velocity_in[:, 0, 0, :]
    moved[...] = jnp.zeros_like(moved)

    row = lax.broadcasted_iota(jnp.int32, (8, atoms), 0)
    iz = iota_f((gz, atoms), 0).astype(BF16)

    def load_cell(step, a, b):
        slot = slot_of(a, b)
        own = slot == OWN
        if step == 0:
            block = packet[...] if own else packets[slot]
            if not own:
                block = jnp.where(exists(a, b), block, 0.0)
            hot[slot] = jnp.where(
                iz == block[2:3].astype(BF16), jnp.ones((), BF16), jnp.zeros((), BF16)
            )
        else:
            block = pk[slot]
            fresh = now[...] if own else jnp.where(exists(a, b), later[slot], 0.0)
            block = jnp.concatenate([block[0:3], fresh, block[6:8]], 0)
        pk[slot] = block
        if abs(a) <= 1:
            base = jnp.where(row == 0, float(a * bx), jnp.where(row == 1, float(b * by), 0.0))
            place = jnp.where(row < 3, block + pltpu.roll(block, 5, 0) + base, 0.0)
            pos[slot] = place
            four = jnp.where(row == 3, 1.0, place) * block[6:7]
            f = jnp.concatenate([*split3(four), jnp.zeros_like(four, BF16)], 0)
            feat[slot] = jnp.concatenate([f, f], 1)
            h, m, l = split3(flat_of(place))
            near_xy[slot] = jnp.concatenate([h, m, h, l, h, m], 0)
            if step == 0:
                rate = 1.0 / (SPREAD * (type_width + block[7:8]))
                near_type[slot] = jnp.concatenate(split3(rate), 0)

    def flat_of(place):
        x = place[0:1] - 0.5 * bx
        y = place[1:2] - 0.5 * by
        return jnp.where(
            row == 0, x, jnp.where(row == 1, y, jnp.where(row == 2, x * x + y * y, jnp.where(row == 3, 1.0, 0.0)))
        )

    types = table.shape[1]
    type_row = lax.broadcasted_iota(jnp.int32, (types, atoms), 0)
    type_width = jnp.zeros((types, atoms), F32)
    for t in range(types):
        type_width = jnp.where(type_row == t, table[1, t] * table[1, t], type_width)

    def own_side(step):
        p = flat_of(pos[OWN])
        turned = jnp.where(
            row < 2, -2.0 * p, jnp.where(row == 2, 1.0, jnp.where(row == 3, p[2:3], 0.0))
        )
        h, m, l = split3(turned)
        rows = jnp.concatenate([h, h, m, h, l, m], 0).astype(F32)
        side_xy[...] = jnp.transpose(rows).astype(BF16)
        col_z[...] = jnp.broadcast_to(jnp.transpose(pos[OWN])[:, 2:3], (atoms, 128))
        if step == 0:
            match = jnp.where(type_row == kinds_in[0], 1.0, 0.0)
            side_type[...] = jnp.transpose(jnp.concatenate([match] * 3, 0)).astype(BF16)

    def squares(step, slot, xy):
        xy[...] = dot_nn(side_xy[...], near_xy[slot])
        if step == 0:
            rates[slot - FIRST] = dot_nn(side_type[...], near_type[slot])

    tall = min(64, atoms)

    def values(slot, xy, tile):
        for k in range(0, atoms, 128):
            z = pos[slot, 2:3, k : k + 128]
            for r in range(0, atoms, tall):
                rows, at = slice(r, r + tall), slice(k, k + 128)
                dz = col_z[rows] - z
                rate = rates[slot - FIRST, rows, at]
                value = jnp.exp2((xy[rows, at] + dz * dz) * rate) * rate
                hi, lo = split2(value)
                tile[rows, at] = hi
                tile[rows, atoms + k : atoms + k + 128] = lo

    def multiply(slot, tile):
        acc[...] += dot_nt(feat[slot], tile[...])

    def near_slot(k):
        slot = FIRST + k
        return slot + (slot >= OWN).astype(jnp.int32)

    def spread(a, b):
        p0 = max(0, a * bx)
        p1 = min(rx, a * bx + bx + 5)
        r0, r1 = {-1: (0, 8), 0: (0, ry), 1: (by, ry)}[b]
        slot = slot_of(a, b)
        block = pk[slot]
        charge = block[6:7]
        ax, ay = block[0:1], block[1:2]
        fx, fy, fz = block[3:4], block[4:5], block[5:6]
        ax = ax + float(a * bx)
        ay = ay + float(b * by)
        in_x = ax + 1.0 + (s * bx).astype(F32) < float(n_x)
        in_y = ay + 1.0 + (q * by).astype(F32) < float(n_y)
        ux = jnp.where(in_x, fx, 0.0)
        uy = jnp.where(in_y, fy, 0.0)
        tx = iota_f((p1 - p0, atoms), 0) + float(p0 - 2) - ax
        wx = tap_of(tx) * (1.0 - fx) + tap_of(tx - 1.0) * ux
        ty = iota_f((r1 - r0, atoms), 0) + float(r0 - 2) - ay
        wy = tap_of(ty) * (1.0 - fy) + tap_of(ty - 1.0) * uy
        low, up = charge * (1.0 - fz), charge * fz
        planes = []
        for w in (wx * low, wx * up):
            plane = jnp.concatenate([wy * w[p : p + 1] for p in range(p1 - p0)], 0)
            planes.extend(split2(plane))
        size = planes[0].shape[0]
        out = dot_nt(jnp.concatenate(planes, 0), hot[slot])
        shape = (p1 - p0, r1 - r0, gz)
        dens[p0:p1, r0:r1] += (out[:size] + out[size : 2 * size]).reshape(shape)
        dens_up[p0:p1, r0:r1] += (out[2 * size : 3 * size] + out[3 * size :]).reshape(shape)

    i = lax.broadcasted_iota(jnp.int32, (gz, gz), 0)
    j = lax.broadcasted_iota(jnp.int32, (gz, gz), 1)
    blur_z = tap_of((i - j).astype(F32)).astype(BF16)
    blur_up = tap_of((i + 1 - j).astype(F32)).astype(BF16)

    def z_blur(x, matrix):
        h, l = split2(x)
        size = x.shape[0]
        both = dot_nn(jnp.concatenate([h, l], 0), matrix)
        return both[:size] + both[size:]

    gx = lax.broadcasted_iota(jnp.int32, (rx, ry, gz), 0) - 2 + s * bx
    gy = lax.broadcasted_iota(jnp.int32, (rx, ry, gz), 1) - 2 + q * by
    inside = (gx >= 0) & (gx < n_x) & (gy >= 0) & (gy < n_y)

    def scales():
        wxp, wyp = bx + 13, by + 16
        tx = lax.broadcasted_iota(jnp.int32, (wxp, wyp, gz), 0) - 6 + s * bx
        ty = lax.broadcasted_iota(jnp.int32, (wxp, wyp, gz), 1) - 8 + q * by
        valid = (tx >= 0) & (tx < n_x) & (ty >= 0) & (ty < n_y)
        t = jnp.where(valid, wide[...], 0.0)
        box_z = band(gz, 4, False)

        def boxed(v):
            two = v[:-1] + v[1:]
            four = two[:-2] + two[2:]
            eight = four[:-4] + four[4:]
            v = eight[:rx] + v[8 : 8 + rx]
            size = wyp
            two = v + pltpu.roll(v, size - 1, 1)
            four = two + pltpu.roll(two, size - 2, 1)
            eight = four + pltpu.roll(four, size - 4, 1)
            nine = eight + pltpu.roll(v, size - 8, 1)
            v = pltpu.roll(nine, size - 2, 1)[:, :ry]
            v = v.reshape(rx * ry, gz)
            h, m, l = split3(v)
            size = v.shape[0]
            out = dot_nn(jnp.concatenate([h, m, l], 0), box_z)
            out = out[:size] + out[size : 2 * size] + out[2 * size :]
            return out.reshape(rx, ry, gz) * (1.0 / 729.0)

        mean_one = boxed(t)
        mean_two = boxed(t * t)
        inverse_scale = lax.rsqrt(mean_two - mean_one * mean_one + EPSILON)
        inv_ref[...] = jnp.where(inside, inverse_scale, 0.0)
        tgt_ref[...] = pltpu.roll(t[4 : 4 + rx], wyp - 6, 1)[:, :ry]

    def map_part():
        size = rx * ry
        blurred = z_blur(dens[...].reshape(size, gz), blur_z)
        blurred = blurred + z_blur(dens_up[...].reshape(size, gz), blur_up)
        blurred = blurred.reshape(rx, ry, gz)
        residual = jnp.where(inside, (blurred - tgt_ref[...]) * inv_ref[...], 0.0)
        along = TAPS[0] * (residual[0 : bx + 1] + residual[4 : bx + 5])
        along = along + TAPS[1] * (residual[1 : bx + 2] + residual[3 : bx + 4])
        along = along + TAPS[2] * residual[2 : bx + 3]
        down = TAPS[0] * along
        for k in range(1, 5):
            down = down + TAPS[k] * pltpu.roll(along, ry - k, 1)
        return z_blur(down.reshape((bx + 1) * ry, gz), blur_z).reshape(bx + 1, ry, gz)

    def gradient_of(potential):
        px = lax.broadcasted_iota(jnp.int32, (bx + 1, ry, gz), 0) + s * bx
        py = lax.broadcasted_iota(jnp.int32, (bx + 1, ry, gz), 1) + q * by
        py_local = lax.broadcasted_iota(jnp.int32, (bx + 1, ry, gz), 1)
        field = jnp.where((px < n_x) & (py < n_y) & (py_local <= by), potential, 0.0)
        own = pk[OWN]
        ax, ay = own[0:1], own[1:2]
        fx, fy, fz = own[3:4], own[4:5], own[5:6]
        size = (bx + 1) * ry
        field = field.reshape(size, gz)
        up = pltpu.roll(field, gz - 1, 1)
        out = dot_nn(jnp.concatenate(split2(field) + split2(up), 0), hot[OWN])
        at_low = out[:size] + out[size : 2 * size]
        slope = out[2 * size : 3 * size] + out[3 * size :] - at_low
        value = at_low + fz * slope
        iy = iota_f((ry, atoms), 0)
        low_y = jnp.where(iy == ay, 1.0, 0.0)
        up_y = jnp.where(iy == ay + 1.0, 1.0, 0.0)
        wy = low_y * (1.0 - fy) + up_y * fy
        sy = up_y - low_y
        grad_x = jnp.zeros((1, atoms), F32)
        grad_y = jnp.zeros((1, atoms), F32)
        grad_z = jnp.zeros((1, atoms), F32)
        for p in range(bx + 1):
            low_x = jnp.where(ax == float(p), 1.0, 0.0)
            up_x = jnp.where(ax + 1.0 == float(p), 1.0, 0.0)
            wx = low_x * (1.0 - fx) + up_x * fx
            sx = up_x - low_x
            v = value[p * ry : (p + 1) * ry]
            g = slope[p * ry : (p + 1) * ry]
            grad_x = grad_x + sx * jnp.sum(wy * v, 0, keepdims=True)
            grad_y = grad_y + wx * jnp.sum(sy * v, 0, keepdims=True)
            grad_z = grad_z + wx * jnp.sum(wy * g, 0, keepdims=True)
        return own[6:7] * jnp.concatenate([grad_x, grad_y, grad_z], 0)

    for step in range(steps):
        last = step == steps - 1
        group = 0 if step == 0 else step + 1
        source, landing = (packet, packets) if step == 0 else (now, later)
        load_cell(step, 0, 0)
        own_side(step)
        acc[...] = jnp.zeros_like(acc)
        dens[...] = jnp.zeros_like(dens)
        dens_up[...] = jnp.zeros_like(dens_up)
        squares(step, OWN, xy0)
        values(OWN, xy0, tile0)
        spread(0, 0)
        each(near, lambda a, b: packet_copy(source, landing, group, a, b, False).wait_recv())
        if step == 0:
            each(others, lambda a, b: target_copy(a, b, True).start())
        for a, b in near:
            load_cell(step, a, b)

        def two_slots(k, carry):
            before = jnp.where(k == 0, OWN, near_slot(2 * k - 1))
            one, two = near_slot(2 * k), near_slot(2 * k + 1)
            squares(step, one, xy1)
            squares(step, two, xy0)
            multiply(before, tile0)
            values(one, xy1, tile1)
            multiply(one, tile1)
            values(two, xy0, tile0)
            return carry

        lax.fori_loop(0, len(near) // 2, two_slots, 0)
        multiply(near_slot(jnp.int32(len(near) - 1)), tile0)
        each(far, lambda a, b: packet_copy(source, landing, group, a, b, False).wait_recv())
        for a, b in far:
            load_cell(step, a, b)
        for a, b in others:
            spread(a, b)
        if step == 0:
            each(others, lambda a, b: target_copy(a, b, False).wait_recv())
            scales()
        potential = map_part()
        if last:
            pot[...] = potential[:bx, :by]
        gradient = gradient_of(potential)
        sums = acc[...]
        sums = sums[0:8] + sums[8:16] + sums[16:24]
        here = pos[OWN][0:3]
        pair = (SPREAD * pk[OWN][6:7]) * (here * sums[3:4] - sums[0:3])
        new_velocity = vel[...] + TIME_STEP * (pair - gradient) / mass[...]
        new_moved = moved[...] + TIME_STEP * new_velocity
        if last:
            vel_out[...] = new_velocity
            moved_out[...] = new_moved
        else:
            vel[...] = new_velocity
            moved[...] = new_moved
            now[...] = pk[OWN][3:6] + TIME_STEP * new_velocity
            each(others, lambda a, b: packet_copy(now, later, step + 2, a, b, True).start())

    each(others, lambda a, b: packet_copy(packet, packets, 0, a, b, True).wait_send())
    each(others, lambda a, b: target_copy(a, b, True).wait_send())
    for step in range(1, steps):
        each(others, lambda a, b: packet_copy(now, later, step + 1, a, b, True).wait_send())


STEPS = 2


def finish(counts, vel, moved, pot, vel_out, moved_out, pot_out):
    live = lax.broadcasted_iota(jnp.int32, vel.shape, 1) < counts[0, 0]
    vel_out[:, 0, 0, :] = jnp.where(live, vel[...], 0.0)
    moved_out[:, 0, 0, :] = jnp.where(live, moved[...], 0.0)
    pot_out[...] = pot[...]


def in_hbm(x):
    return pltpu.with_memory_space_constraint(x, pltpu.HBM)


def per_device(fraction, velocity, anchor, atom_types, counts, type_table, target):
    atoms = fraction.shape[3]
    bx, by, gz = target.shape
    types = type_table.shape[1]
    n_x = bx * lax.axis_size("cells")
    n_y = by * lax.axis_size("grp")
    row = jax.ShapeDtypeStruct((3, atoms), F32)
    final = jax.ShapeDtypeStruct(velocity.shape, F32)
    field = jax.ShapeDtypeStruct((bx, by, gz), F32)
    region = pltpu.VMEM((bx + 5, by + 8, gz), F32)
    three = pltpu.VMEM((3, atoms), F32)
    square = pltpu.VMEM((atoms, atoms), F32)
    tile = pltpu.VMEM((atoms, 2 * atoms), BF16)
    done = pl.pallas_call(
        functools.partial(kernel, STEPS, bx, by, gz, n_x, n_y),
        out_shape=[row, row, field],
        in_specs=[HBM, HBM, HBM, HBM, SMEM, HBM, HBM],
        out_specs=[VMEM] * 3,
        scratch_shapes=[
            pltpu.VMEM(fraction.shape, F32),
            pltpu.VMEM(velocity.shape, F32),
            pltpu.VMEM(anchor.shape, jnp.int32),
            pltpu.VMEM(atom_types.shape, jnp.int32),
            pltpu.SMEM(type_table.shape, F32),
            pltpu.VMEM((8, atoms), F32),
            pltpu.VMEM((1, atoms), F32),
            pltpu.VMEM((SLOTS, 8, atoms), F32),
            pltpu.VMEM((bx + 13, by + 16, gz), F32),
            three,
            pltpu.VMEM((SLOTS, 3, atoms), F32),
            three,
            three,
            pltpu.VMEM((SLOTS, 8, atoms), F32),
            pltpu.VMEM((SLOTS, 8, atoms), F32),
            pltpu.VMEM((SLOTS, 32, 2 * atoms), BF16),
            pltpu.VMEM((SLOTS, gz, atoms), BF16),
            pltpu.VMEM((atoms, 48), BF16),
            pltpu.VMEM((atoms, 3 * types), BF16),
            pltpu.VMEM((SLOTS, 48, atoms), BF16),
            pltpu.VMEM((SLOTS, 3 * types, atoms), BF16),
            pltpu.VMEM((atoms, 128), F32),
            square,
            square,
            pltpu.VMEM((3 * NB, atoms, atoms), F32),
            tile,
            tile,
            pltpu.VMEM((32, atoms), F32),
            region,
            region,
            region,
            region,
            pltpu.SemaphoreType.DMA((STEPS + 1, SLOTS)),
            pltpu.SemaphoreType.DMA((STEPS + 1, SLOTS)),
            pltpu.SemaphoreType.DMA((6,)),
        ],
        compiler_params=pltpu.CompilerParams(
            collective_id=0, has_side_effects=True, vmem_limit_bytes=40 * 2**20
        ),
        name="dynamics",
    )(*map(in_hbm, (fraction, velocity, anchor, atom_types)), counts, in_hbm(type_table), in_hbm(target))
    return tuple(
        pl.pallas_call(
            finish,
            out_shape=[final, final, field],
            in_specs=[SMEM, VMEM, VMEM, VMEM],
            out_specs=[VMEM] * 3,
            compiler_params=pltpu.CompilerParams(vmem_limit_bytes=4 * 2**20),
            name="finish",
        )(counts, *done)
    )


def solution(mesh):
    placed = (
        P(None, "cells", "grp", None),
        P(None, "cells", "grp", None),
        P(None, "cells", "grp", None),
        P("cells", "grp", None),
        P("cells", "grp"),
        P(),
        P("cells", "grp", None),
    )
    return jax.shard_map(
        per_device,
        mesh=mesh,
        in_specs=placed,
        out_specs=(
            P(None, "cells", "grp", None),
            P(None, "cells", "grp", None),
            P("cells", "grp", None),
        ),
        check_vma=False,
    )
```

```python
import functools
import math

import jax
import jax.numpy as jnp
from jax import lax
from jax.experimental import pallas as pl
from jax.experimental.pallas import tpu as pltpu
from jax.sharding import PartitionSpec as P

EPSILON = 1e-06
TIME_STEP = 0.5
TAPS = (1.0 / 16.0, 4.0 / 16.0, 6.0 / 16.0, 4.0 / 16.0, 1.0 / 16.0)
F32 = jnp.float32
BF16 = jnp.bfloat16
RX, RY = 2, 1
NB = 2 * RY + 1
SLOTS = (2 * RX + 1) * NB
OWN = RX * NB + RY
MESH = pl.DeviceIdType.MESH
VMEM = pl.BlockSpec(memory_space=pltpu.VMEM)
SMEM = pl.BlockSpec(memory_space=pltpu.SMEM)
HBM = pl.BlockSpec(memory_space=pltpu.HBM)
NEIGHBOURS = tuple(
    (a, b) for a in range(-RX, RX + 1) for b in range(-RY, RY + 1) if (a, b) != (0, 0)
)


def slot_of(a, b):
    return (a + RX) * NB + (b + RY)


def exists(a, b):
    s = lax.axis_index("cells") + a
    q = lax.axis_index("grp") + b
    ns, nq = lax.axis_size("cells"), lax.axis_size("grp")
    return (s >= 0) & (s < ns) & (q >= 0) & (q < nq)


def target_piece(a, b, bx, by):
    x0 = max(0, -6 - a * bx)
    x1 = min(bx, bx + 7 - a * bx)
    y0, y1 = {-1: (by - 8, by), 0: (0, by), 1: (0, 8)}[b]
    return x0, x1, y0, y1


def split2(x):
    hi = x.astype(BF16)
    return hi, (x - hi.astype(F32)).astype(BF16)


def split3(x):
    hi = x.astype(BF16)
    rest = x - hi.astype(F32)
    mid = rest.astype(BF16)
    return hi, mid, (rest - mid.astype(F32)).astype(BF16)


def dot_nn(x, y):
    return lax.dot_general(x, y, (((1,), (0,)), ((), ())), preferred_element_type=F32)


def dot_nt(x, y):
    return lax.dot_general(x, y, (((1,), (1,)), ((), ())), preferred_element_type=F32)


def iota_f(shape, dim):
    return lax.broadcasted_iota(jnp.int32, shape, dim).astype(F32)


def tap_of(t):
    u = jnp.abs(t)
    return jnp.where(
        u == 0.0, TAPS[2], jnp.where(u == 1.0, TAPS[1], jnp.where(u == 2.0, TAPS[0], 0.0))
    )


def band(gz, radius, taps):
    i = lax.broadcasted_iota(jnp.int32, (gz, gz), 0)
    j = lax.broadcasted_iota(jnp.int32, (gz, gz), 1)
    t = (i - j).astype(F32)
    if taps:
        return tap_of(t).astype(BF16)
    return jnp.where(jnp.abs(t) <= radius, 1.0, 0.0).astype(BF16)


def pack(fraction, anchor, kinds, counts, table, packet, mass):
    atoms = packet.shape[1]
    n = counts[0, 0]
    kind = kinds[0]
    lane = lax.broadcasted_iota(jnp.int32, (1, atoms), 1)
    rows = []
    for r in range(3):
        row = jnp.zeros((1, atoms), F32)
        for t in range(table.shape[1]):
            row = jnp.where(kind == t, table[r, t], row)
        rows.append(row)
    packet[0:3] = anchor[:, 0, 0, :].astype(F32)
    packet[3:6] = fraction[:, 0, 0, :]
    packet[6:7] = jnp.where(lane < n, rows[0], 0.0)
    packet[7:8] = rows[1] * rows[1]
    mass[...] = rows[2]


SPREAD = -2.0 / math.log2(math.e)
FIRST = NB * (RX - 1)


def kernel(steps, bx, by, gz, n_x, n_y, *refs):
    (fraction, velocity, anchor, kinds, own_counts, table_hbm, target,
     vel_out, moved_out, pot,
     fraction_in, velocity_in, anchor_in, kinds_in, table, packet, mass, packets, wide, now, later, vel, moved,
     pk, pos, feat, hot, side_xy, side_type, near_xy, near_type, col_z, xy0, xy1, rates,
     acc, dens, dens_up, inv_ref, tgt_ref,
     send_sem, recv_sem, load_sem) = refs
    atoms = packet.shape[1]
    s, q = lax.axis_index("cells"), lax.axis_index("grp")
    rx, ry = bx + 5, by + 8
    near = [(a, b) for a, b in NEIGHBOURS if abs(a) <= 1]
    far = [(a, b) for a, b in NEIGHBOURS if abs(a) > 1]
    others = near + far

    barrier = pltpu.get_barrier_semaphore()
    total = jnp.int32(0)
    for a, b in NEIGHBOURS:
        there = exists(a, b)
        total = total + there.astype(jnp.int32)

        @pl.when(there)
        def _(a=a, b=b):
            pl.semaphore_signal(barrier, inc=1, device_id=(s + a, q + b), device_id_type=MESH)

    own_target = wide.at[6 : 6 + bx, 8 : 8 + by]
    loads = [
        pltpu.make_async_copy(src, dst, load_sem.at[k])
        for k, (src, dst) in enumerate(
            [(anchor, anchor_in), (fraction, fraction_in), (kinds, kinds_in), (table_hbm, table),
             (velocity, velocity_in), (target, own_target)]
        )
    ]
    for load in loads:
        load.start()
    for load in loads[:4]:
        load.wait()
    pack(fraction_in, anchor_in, kinds_in, own_counts, table, packet, mass)
    pl.semaphore_wait(barrier, total)

    def packet_copy(src, dst, group, a, b, there):
        mine, back = slot_of(a, b), slot_of(-a, -b)
        slot = back if there else mine
        return pltpu.make_async_remote_copy(
            src_ref=src,
            dst_ref=dst.at[slot],
            send_sem=send_sem.at[group, mine],
            recv_sem=recv_sem.at[group, slot],
            device_id=(s + a, q + b),
            device_id_type=MESH,
        )

    def target_copy(a, b, there):
        mine, back = slot_of(a, b), slot_of(-a, -b)
        slot = back if there else mine
        c, d = (-a, -b) if there else (a, b)
        x0, x1, y0, y1 = target_piece(c, d, bx, by)
        X, Y = 6 + c * bx + x0, 8 + d * by + y0
        return pltpu.make_async_remote_copy(
            src_ref=target.at[x0:x1, y0:y1],
            dst_ref=wide.at[X : X + x1 - x0, Y : Y + y1 - y0],
            send_sem=send_sem.at[1, mine],
            recv_sem=recv_sem.at[1, slot],
            device_id=(s + a, q + b),
            device_id_type=MESH,
        )

    def each(cells, act):
        for a, b in cells:

            @pl.when(exists(a, b))
            def _(a=a, b=b):
                act(a, b)

    each(others, lambda a, b: packet_copy(packet, packets, 0, a, b, True).start())
    for load in loads[4:]:
        load.wait()
    vel[...] = velocity_in[:, 0, 0, :]
    moved[...] = jnp.zeros_like(moved)

    row = lax.broadcasted_iota(jnp.int32, (8, atoms), 0)
    iz = iota_f((gz, atoms), 0).astype(BF16)

    def load_cell(step, a, b):
        slot = slot_of(a, b)
        own = isinstance(slot, int) and slot == OWN
        if step == 0:
            block = packet[...] if own else packets[slot]
            if not own:
                block = jnp.where(exists(a, b), block, 0.0)
            hot[slot] = jnp.where(
                iz == block[2:3].astype(BF16), jnp.ones((), BF16), jnp.zeros((), BF16)
            )
        else:
            block = pk[slot]
            fresh = now[...] if own else jnp.where(exists(a, b), later[slot], 0.0)
            block = jnp.concatenate([block[0:3], fresh, block[6:8]], 0)
        pk[slot] = block
        return slot, block

    def load_near(step, a, b):
        slot, block = load_cell(step, a, b)
        base_x = jnp.asarray(a * bx, F32)
        base_y = jnp.asarray(b * by, F32)
        base = jnp.where(row == 0, base_x, jnp.where(row == 1, base_y, 0.0))
        place = jnp.where(row < 3, block + pltpu.roll(block, 5, 0) + base, 0.0)
        pos[slot] = place
        feat[slot] = jnp.where(row == 3, 1.0, place) * block[6:7]
        h, m, l = split3(flat_of(place))
        near_xy[slot] = jnp.concatenate([h, m, h, l, h, m], 0)
        if step == 0:
            rate = 1.0 / (SPREAD * (type_width + block[7:8]))
            near_type[slot] = jnp.concatenate(split3(rate), 0)
        return slot

    def flat_of(place):
        x = place[0:1] - 0.5 * bx
        y = place[1:2] - 0.5 * by
        return jnp.where(
            row == 0, x, jnp.where(row == 1, y, jnp.where(row == 2, x * x + y * y, jnp.where(row == 3, 1.0, 0.0)))
        )

    types = table.shape[1]
    type_row = lax.broadcasted_iota(jnp.int32, (types, atoms), 0)
    type_width = jnp.zeros((types, atoms), F32)
    for t in range(types):
        type_width = jnp.where(type_row == t, table[1, t] * table[1, t], type_width)

    def own_side(step):
        p = flat_of(pos[OWN])
        turned = jnp.where(
            row < 2, -2.0 * p, jnp.where(row == 2, 1.0, jnp.where(row == 3, p[2:3], 0.0))
        )
        h, m, l = split3(turned)
        rows = jnp.concatenate([h, h, m, h, l, m], 0).astype(F32)
        side_xy[...] = jnp.transpose(rows).astype(BF16)
        col_z[...] = jnp.broadcast_to(jnp.transpose(pos[OWN])[:, 2:3], (atoms, 128))
        if step == 0:
            match = jnp.where(type_row == kinds_in[0], 1.0, 0.0)
            side_type[...] = jnp.transpose(jnp.concatenate([match] * 3, 0)).astype(BF16)

    def squares(step, slot, xy):
        xy[...] = dot_nn(side_xy[...], near_xy[slot])
        if step == 0:
            rates[slot - FIRST] = dot_nn(side_type[...], near_type[slot])

    tall = min(16, atoms)

    def values(*pairs):
        for r in range(0, atoms, tall):
            rows = slice(r, r + tall)
            z = col_z[rows]
            sums = [acc[f, rows] for f in range(4)]
            for slot, xy in pairs:
                for k in range(0, atoms, 128):
                    at = slice(k, k + 128)
                    dz = z - pos[slot, 2:3, at]
                    rate = rates[slot - FIRST, rows, at]
                    value = jnp.exp2((xy[rows, at] + dz * dz) * rate) * rate
                    for f in range(4):
                        sums[f] = sums[f] + value * feat[slot, f : f + 1, at]
            for f in range(4):
                acc[f, rows] = sums[f]

    def spread(a, b):
        p0 = max(0, a * bx)
        p1 = min(rx, a * bx + bx + 5)
        r0, r1 = {-1: (0, 8), 0: (0, ry), 1: (by, ry)}[b]
        slot = slot_of(a, b)
        block = pk[slot]
        charge = block[6:7]
        ax, ay = block[0:1], block[1:2]
        fx, fy, fz = block[3:4], block[4:5], block[5:6]
        ax = ax + float(a * bx)
        ay = ay + float(b * by)
        in_x = ax + 1.0 + (s * bx).astype(F32) < float(n_x)
        in_y = ay + 1.0 + (q * by).astype(F32) < float(n_y)
        ux = jnp.where(in_x, fx, 0.0)
        uy = jnp.where(in_y, fy, 0.0)
        tx = iota_f((p1 - p0, atoms), 0) + float(p0 - 2) - ax
        wx = tap_of(tx) * (1.0 - fx) + tap_of(tx - 1.0) * ux
        ty = iota_f((r1 - r0, atoms), 0) + float(r0 - 2) - ay
        wy = tap_of(ty) * (1.0 - fy) + tap_of(ty - 1.0) * uy
        low, up = charge * (1.0 - fz), charge * fz
        planes = []
        for w in (wx * low, wx * up):
            plane = jnp.concatenate([wy * w[p : p + 1] for p in range(p1 - p0)], 0)
            planes.extend(split2(plane))
        size = planes[0].shape[0]
        out = dot_nt(jnp.concatenate(planes, 0), hot[slot])
        shape = (p1 - p0, r1 - r0, gz)
        dens[p0:p1, r0:r1] += (out[:size] + out[size : 2 * size]).reshape(shape)
        dens_up[p0:p1, r0:r1] += (out[2 * size : 3 * size] + out[3 * size :]).reshape(shape)

    i = lax.broadcasted_iota(jnp.int32, (gz, gz), 0)
    j = lax.broadcasted_iota(jnp.int32, (gz, gz), 1)
    blur_z = tap_of((i - j).astype(F32)).astype(BF16)
    blur_up = tap_of((i + 1 - j).astype(F32)).astype(BF16)

    def z_blur(x, matrix):
        h, l = split2(x)
        size = x.shape[0]
        both = dot_nn(jnp.concatenate([h, l], 0), matrix)
        return both[:size] + both[size:]

    gx = lax.broadcasted_iota(jnp.int32, (rx, ry, gz), 0) - 2 + s * bx
    gy = lax.broadcasted_iota(jnp.int32, (rx, ry, gz), 1) - 2 + q * by
    inside = (gx >= 0) & (gx < n_x) & (gy >= 0) & (gy < n_y)

    def scales():
        wxp, wyp = bx + 13, by + 16
        tx = lax.broadcasted_iota(jnp.int32, (wxp, wyp, gz), 0) - 6 + s * bx
        ty = lax.broadcasted_iota(jnp.int32, (wxp, wyp, gz), 1) - 8 + q * by
        valid = (tx >= 0) & (tx < n_x) & (ty >= 0) & (ty < n_y)
        t = jnp.where(valid, wide[...], 0.0)
        box_z = band(gz, 4, False)

        def boxed(v):
            two = v[:-1] + v[1:]
            four = two[:-2] + two[2:]
            eight = four[:-4] + four[4:]
            v = eight[:rx] + v[8 : 8 + rx]
            size = wyp
            two = v + pltpu.roll(v, size - 1, 1)
            four = two + pltpu.roll(two, size - 2, 1)
            eight = four + pltpu.roll(four, size - 4, 1)
            nine = eight + pltpu.roll(v, size - 8, 1)
            v = pltpu.roll(nine, size - 2, 1)[:, :ry]
            v = v.reshape(rx * ry, gz)
            h, m, l = split3(v)
            size = v.shape[0]
            out = dot_nn(jnp.concatenate([h, m, l], 0), box_z)
            out = out[:size] + out[size : 2 * size] + out[2 * size :]
            return out.reshape(rx, ry, gz) * (1.0 / 729.0)

        mean_one = boxed(t)
        mean_two = boxed(t * t)
        inverse_scale = lax.rsqrt(mean_two - mean_one * mean_one + EPSILON)
        inv_ref[...] = jnp.where(inside, inverse_scale, 0.0)
        tgt_ref[...] = pltpu.roll(t[4 : 4 + rx], wyp - 6, 1)[:, :ry]

    def map_part():
        size = rx * ry
        blurred = z_blur(dens[...].reshape(size, gz), blur_z)
        blurred = blurred + z_blur(dens_up[...].reshape(size, gz), blur_up)
        blurred = blurred.reshape(rx, ry, gz)
        residual = jnp.where(inside, (blurred - tgt_ref[...]) * inv_ref[...], 0.0)
        along = TAPS[0] * (residual[0 : bx + 1] + residual[4 : bx + 5])
        along = along + TAPS[1] * (residual[1 : bx + 2] + residual[3 : bx + 4])
        along = along + TAPS[2] * residual[2 : bx + 3]
        down = TAPS[0] * along
        for k in range(1, 5):
            down = down + TAPS[k] * pltpu.roll(along, ry - k, 1)
        return z_blur(down.reshape((bx + 1) * ry, gz), blur_z).reshape(bx + 1, ry, gz)

    def gradient_of(potential):
        px = lax.broadcasted_iota(jnp.int32, (bx + 1, ry, gz), 0) + s * bx
        py = lax.broadcasted_iota(jnp.int32, (bx + 1, ry, gz), 1) + q * by
        py_local = lax.broadcasted_iota(jnp.int32, (bx + 1, ry, gz), 1)
        field = jnp.where((px < n_x) & (py < n_y) & (py_local <= by), potential, 0.0)
        own = pk[OWN]
        ax, ay = own[0:1], own[1:2]
        fx, fy, fz = own[3:4], own[4:5], own[5:6]
        size = (bx + 1) * ry
        field = field.reshape(size, gz)
        up = pltpu.roll(field, gz - 1, 1)
        out = dot_nn(jnp.concatenate(split2(field) + split2(up), 0), hot[OWN])
        at_low = out[:size] + out[size : 2 * size]
        slope = out[2 * size : 3 * size] + out[3 * size :] - at_low
        value = at_low + fz * slope
        iy = iota_f((ry, atoms), 0)
        low_y = jnp.where(iy == ay, 1.0, 0.0)
        up_y = jnp.where(iy == ay + 1.0, 1.0, 0.0)
        wy = low_y * (1.0 - fy) + up_y * fy
        sy = up_y - low_y
        grad_x = jnp.zeros((1, atoms), F32)
        grad_y = jnp.zeros((1, atoms), F32)
        grad_z = jnp.zeros((1, atoms), F32)
        for p in range(bx + 1):
            low_x = jnp.where(ax == float(p), 1.0, 0.0)
            up_x = jnp.where(ax + 1.0 == float(p), 1.0, 0.0)
            wx = low_x * (1.0 - fx) + up_x * fx
            sx = up_x - low_x
            v = value[p * ry : (p + 1) * ry]
            g = slope[p * ry : (p + 1) * ry]
            grad_x = grad_x + sx * jnp.sum(wy * v, 0, keepdims=True)
            grad_y = grad_y + wx * jnp.sum(sy * v, 0, keepdims=True)
            grad_z = grad_z + wx * jnp.sum(wy * g, 0, keepdims=True)
        return own[6:7] * jnp.concatenate([grad_x, grad_y, grad_z], 0)

    for step in range(steps):
        last = step == steps - 1
        group = 0 if step == 0 else step + 1
        source, landing = (packet, packets) if step == 0 else (now, later)
        load_near(step, 0, 0)
        own_side(step)
        acc[...] = jnp.zeros_like(acc)
        dens[...] = jnp.zeros_like(dens)
        dens_up[...] = jnp.zeros_like(dens_up)
        squares(step, OWN, xy0)
        values((OWN, xy0))
        spread(0, 0)

        def two_cells(k, carry):
            da = jnp.minimum(k, 1)
            db = jnp.where(k == 1, 0, jnp.where(k == 3, -1, 1))
            each([(-da, -db), (da, db)], lambda a, b: packet_copy(source, landing, group, a, b, False).wait_recv())

            if step == 0:

                @pl.when(k == 0)
                def _():
                    each(others, lambda a, b: target_copy(a, b, True).start())

            one = load_near(step, -da, -db)
            two = load_near(step, da, db)
            squares(step, one, xy0)
            squares(step, two, xy1)
            values((one, xy0), (two, xy1))
            return carry

        lax.fori_loop(0, len(near) // 2, two_cells, 0)
        each(far, lambda a, b: packet_copy(source, landing, group, a, b, False).wait_recv())
        for a, b in far:
            load_cell(step, a, b)
        for a, b in others:
            spread(a, b)
        if step == 0:
            each(others, lambda a, b: target_copy(a, b, False).wait_recv())
            scales()
        potential = map_part()
        if last:
            pot[...] = potential[:bx, :by]
        gradient = gradient_of(potential)
        lane = lax.broadcasted_iota(jnp.int32, (atoms, 128), 1)
        turned = jnp.zeros((atoms, 128), F32)
        for f in range(4):
            turned = jnp.where(lane == f, jnp.sum(acc[f], 1, keepdims=True), turned)
        sums = jnp.transpose(turned)[0:8]
        here = pos[OWN][0:3]
        pair = (SPREAD * pk[OWN][6:7]) * (here * sums[3:4] - sums[0:3])
        new_velocity = vel[...] + TIME_STEP * (pair - gradient) / mass[...]
        new_moved = moved[...] + TIME_STEP * new_velocity
        if last:
            vel_out[...] = new_velocity
            moved_out[...] = new_moved
        else:
            vel[...] = new_velocity
            moved[...] = new_moved
            now[...] = pk[OWN][3:6] + TIME_STEP * new_velocity
            each(others, lambda a, b: packet_copy(now, later, step + 2, a, b, True).start())

    each(others, lambda a, b: packet_copy(packet, packets, 0, a, b, True).wait_send())
    each(others, lambda a, b: target_copy(a, b, True).wait_send())
    for step in range(1, steps):
        each(others, lambda a, b: packet_copy(now, later, step + 1, a, b, True).wait_send())


STEPS = 2


def finish(counts, vel, moved, pot, vel_out, moved_out, pot_out):
    live = lax.broadcasted_iota(jnp.int32, vel.shape, 1) < counts[0, 0]
    vel_out[:, 0, 0, :] = jnp.where(live, vel[...], 0.0)
    moved_out[:, 0, 0, :] = jnp.where(live, moved[...], 0.0)
    pot_out[...] = pot[...]


def in_hbm(x):
    return pltpu.with_memory_space_constraint(x, pltpu.HBM)


def per_device(fraction, velocity, anchor, atom_types, counts, type_table, target):
    atoms = fraction.shape[3]
    bx, by, gz = target.shape
    types = type_table.shape[1]
    n_x = bx * lax.axis_size("cells")
    n_y = by * lax.axis_size("grp")
    row = jax.ShapeDtypeStruct((3, atoms), F32)
    final = jax.ShapeDtypeStruct(velocity.shape, F32)
    field = jax.ShapeDtypeStruct((bx, by, gz), F32)
    region = pltpu.VMEM((bx + 5, by + 8, gz), F32)
    three = pltpu.VMEM((3, atoms), F32)
    square = pltpu.VMEM((atoms, atoms), F32)
    done = pl.pallas_call(
        functools.partial(kernel, STEPS, bx, by, gz, n_x, n_y),
        out_shape=[row, row, field],
        in_specs=[HBM, HBM, HBM, HBM, SMEM, HBM, HBM],
        out_specs=[VMEM] * 3,
        scratch_shapes=[
            pltpu.VMEM(fraction.shape, F32),
            pltpu.VMEM(velocity.shape, F32),
            pltpu.VMEM(anchor.shape, jnp.int32),
            pltpu.VMEM(atom_types.shape, jnp.int32),
            pltpu.SMEM(type_table.shape, F32),
            pltpu.VMEM((8, atoms), F32),
            pltpu.VMEM((1, atoms), F32),
            pltpu.VMEM((SLOTS, 8, atoms), F32),
            pltpu.VMEM((bx + 13, by + 16, gz), F32),
            three,
            pltpu.VMEM((SLOTS, 3, atoms), F32),
            three,
            three,
            pltpu.VMEM((SLOTS, 8, atoms), F32),
            pltpu.VMEM((SLOTS, 8, atoms), F32),
            pltpu.VMEM((SLOTS, 8, atoms), F32),
            pltpu.VMEM((SLOTS, gz, atoms), BF16),
            pltpu.VMEM((atoms, 48), BF16),
            pltpu.VMEM((atoms, 3 * types), BF16),
            pltpu.VMEM((SLOTS, 48, atoms), BF16),
            pltpu.VMEM((SLOTS, 3 * types, atoms), BF16),
            pltpu.VMEM((atoms, 128), F32),
            square,
            square,
            pltpu.VMEM((3 * NB, atoms, atoms), F32),
            pltpu.VMEM((4, atoms, 128), F32),
            region,
            region,
            region,
            region,
            pltpu.SemaphoreType.DMA((STEPS + 1, SLOTS)),
            pltpu.SemaphoreType.DMA((STEPS + 1, SLOTS)),
            pltpu.SemaphoreType.DMA((6,)),
        ],
        compiler_params=pltpu.CompilerParams(
            collective_id=0, has_side_effects=True, vmem_limit_bytes=40 * 2**20
        ),
        name="dynamics",
    )(*map(in_hbm, (fraction, velocity, anchor, atom_types)), counts, in_hbm(type_table), in_hbm(target))
    return tuple(
        pl.pallas_call(
            finish,
            out_shape=[final, final, field],
            in_specs=[SMEM, VMEM, VMEM, VMEM],
            out_specs=[VMEM] * 3,
            compiler_params=pltpu.CompilerParams(vmem_limit_bytes=4 * 2**20),
            name="finish",
        )(counts, *done)
    )


def solution(mesh):
    placed = (
        P(None, "cells", "grp", None),
        P(None, "cells", "grp", None),
        P(None, "cells", "grp", None),
        P("cells", "grp", None),
        P("cells", "grp"),
        P(),
        P("cells", "grp", None),
    )
    return jax.shard_map(
        per_device,
        mesh=mesh,
        in_specs=placed,
        out_specs=(
            P(None, "cells", "grp", None),
            P(None, "cells", "grp", None),
            P("cells", "grp", None),
        ),
        check_vma=False,
    )
```

```python
import functools
import math

import jax
import jax.numpy as jnp
from jax import lax
from jax.experimental import pallas as pl
from jax.experimental.pallas import tpu as pltpu
from jax.sharding import PartitionSpec as P

EPSILON = 1e-06
TIME_STEP = 0.5
TAPS = (1.0 / 16.0, 4.0 / 16.0, 6.0 / 16.0, 4.0 / 16.0, 1.0 / 16.0)
F32 = jnp.float32
BF16 = jnp.bfloat16
RX, RY = 2, 1
NB = 2 * RY + 1
SLOTS = (2 * RX + 1) * NB
OWN = RX * NB + RY
MESH = pl.DeviceIdType.MESH
VMEM = pl.BlockSpec(memory_space=pltpu.VMEM)
SMEM = pl.BlockSpec(memory_space=pltpu.SMEM)
HBM = pl.BlockSpec(memory_space=pltpu.HBM)
NEIGHBOURS = tuple(
    (a, b) for a in range(-RX, RX + 1) for b in range(-RY, RY + 1) if (a, b) != (0, 0)
)


def slot_of(a, b):
    return (a + RX) * NB + (b + RY)


def exists(a, b):
    s = lax.axis_index("cells") + a
    q = lax.axis_index("grp") + b
    ns, nq = lax.axis_size("cells"), lax.axis_size("grp")
    return (s >= 0) & (s < ns) & (q >= 0) & (q < nq)


def target_piece(a, b, bx, by):
    x0 = max(0, -6 - a * bx)
    x1 = min(bx, bx + 7 - a * bx)
    y0, y1 = {-1: (by - 8, by), 0: (0, by), 1: (0, 8)}[b]
    return x0, x1, y0, y1


def split2(x):
    hi = x.astype(BF16)
    return hi, (x - hi.astype(F32)).astype(BF16)


def split3(x):
    hi = x.astype(BF16)
    rest = x - hi.astype(F32)
    mid = rest.astype(BF16)
    return hi, mid, (rest - mid.astype(F32)).astype(BF16)


def dot_nn(x, y):
    return lax.dot_general(x, y, (((1,), (0,)), ((), ())), preferred_element_type=F32)


def dot_nt(x, y):
    return lax.dot_general(x, y, (((1,), (1,)), ((), ())), preferred_element_type=F32)


def iota_f(shape, dim):
    return lax.broadcasted_iota(jnp.int32, shape, dim).astype(F32)


def tap_of(t):
    u = jnp.abs(t)
    return jnp.where(
        u == 0.0, TAPS[2], jnp.where(u == 1.0, TAPS[1], jnp.where(u == 2.0, TAPS[0], 0.0))
    )


def band(gz, radius, taps):
    i = lax.broadcasted_iota(jnp.int32, (gz, gz), 0)
    j = lax.broadcasted_iota(jnp.int32, (gz, gz), 1)
    t = (i - j).astype(F32)
    if taps:
        return tap_of(t).astype(BF16)
    return jnp.where(jnp.abs(t) <= radius, 1.0, 0.0).astype(BF16)


def pack(fraction, anchor, kinds, counts, table, packet, mass):
    atoms = packet.shape[1]
    n = counts[0, 0]
    kind = kinds[0]
    lane = lax.broadcasted_iota(jnp.int32, (1, atoms), 1)
    rows = []
    for r in range(3):
        row = jnp.zeros((1, atoms), F32)
        for t in range(table.shape[1]):
            row = jnp.where(kind == t, table[r, t], row)
        rows.append(row)
    packet[0:3] = anchor[:, 0, 0, :].astype(F32)
    packet[3:6] = fraction[:, 0, 0, :]
    packet[6:7] = jnp.where(lane < n, rows[0], 0.0)
    packet[7:8] = rows[1] * rows[1]
    mass[...] = rows[2]


SPREAD = -2.0 / math.log2(math.e)
FIRST = NB * (RX - 1)


def kernel(steps, bx, by, gz, n_x, n_y, *refs):
    (fraction, velocity, anchor, kinds, own_counts, table_hbm, target,
     vel_out, moved_out, pot,
     fraction_in, velocity_in, anchor_in, kinds_in, table, packet, mass, packets, wide, now, later, vel, moved,
     pk, pos, feat, hot, side_xy, side_type, near_xy, near_type, col_z, xy0, xy1, rates,
     acc, dens, dens_up, inv_ref, tgt_ref,
     send_sem, recv_sem, load_sem) = refs
    atoms = packet.shape[1]
    s, q = lax.axis_index("cells"), lax.axis_index("grp")
    rx, ry = bx + 5, by + 8
    near = [(0, -1), (0, 1), (-1, 0), (1, 0), (-1, -1), (1, 1), (-1, 1), (1, -1)]
    far = [(a, b) for a, b in NEIGHBOURS if abs(a) > 1]
    others = near + far

    barrier = pltpu.get_barrier_semaphore()
    total = jnp.int32(0)
    for a, b in NEIGHBOURS:
        there = exists(a, b)
        total = total + there.astype(jnp.int32)

        @pl.when(there)
        def _(a=a, b=b):
            pl.semaphore_signal(barrier, inc=1, device_id=(s + a, q + b), device_id_type=MESH)

    own_target = wide.at[6 : 6 + bx, 8 : 8 + by]
    loads = [
        pltpu.make_async_copy(src, dst, load_sem.at[k])
        for k, (src, dst) in enumerate(
            [(anchor, anchor_in), (fraction, fraction_in), (kinds, kinds_in), (table_hbm, table),
             (velocity, velocity_in), (target, own_target)]
        )
    ]
    for load in loads:
        load.start()
    for load in loads[:4]:
        load.wait()
    pack(fraction_in, anchor_in, kinds_in, own_counts, table, packet, mass)
    pl.semaphore_wait(barrier, total)

    def packet_copy(src, dst, group, a, b, there):
        mine, back = slot_of(a, b), slot_of(-a, -b)
        slot = back if there else mine
        return pltpu.make_async_remote_copy(
            src_ref=src,
            dst_ref=dst.at[slot],
            send_sem=send_sem.at[group, mine],
            recv_sem=recv_sem.at[group, slot],
            device_id=(s + a, q + b),
            device_id_type=MESH,
        )

    def target_copy(a, b, there):
        mine, back = slot_of(a, b), slot_of(-a, -b)
        slot = back if there else mine
        c, d = (-a, -b) if there else (a, b)
        x0, x1, y0, y1 = target_piece(c, d, bx, by)
        X, Y = 6 + c * bx + x0, 8 + d * by + y0
        return pltpu.make_async_remote_copy(
            src_ref=target.at[x0:x1, y0:y1],
            dst_ref=wide.at[X : X + x1 - x0, Y : Y + y1 - y0],
            send_sem=send_sem.at[1, mine],
            recv_sem=recv_sem.at[1, slot],
            device_id=(s + a, q + b),
            device_id_type=MESH,
        )

    def each(cells, act):
        for a, b in cells:

            @pl.when(exists(a, b))
            def _(a=a, b=b):
                act(a, b)

    each(others, lambda a, b: packet_copy(packet, packets, 0, a, b, True).start())
    for load in loads[4:]:
        load.wait()
    vel[...] = velocity_in[:, 0, 0, :]
    moved[...] = jnp.zeros_like(moved)

    row = lax.broadcasted_iota(jnp.int32, (8, atoms), 0)
    iz = iota_f((gz, atoms), 0).astype(BF16)

    def load_cell(step, a, b):
        slot = slot_of(a, b)
        own = isinstance(slot, int) and slot == OWN
        if step == 0:
            block = packet[...] if own else packets[slot]
            if not own:
                block = jnp.where(exists(a, b), block, 0.0)
            hot[slot] = jnp.where(
                iz == block[2:3].astype(BF16), jnp.ones((), BF16), jnp.zeros((), BF16)
            )
        else:
            block = pk[slot]
            fresh = now[...] if own else jnp.where(exists(a, b), later[slot], 0.0)
            block = jnp.concatenate([block[0:3], fresh, block[6:8]], 0)
        pk[slot] = block
        return slot, block

    def load_near(step, a, b):
        slot, block = load_cell(step, a, b)
        base_x = jnp.asarray(a * bx, F32)
        base_y = jnp.asarray(b * by, F32)
        base = jnp.where(row == 0, base_x, jnp.where(row == 1, base_y, 0.0))
        place = jnp.where(row < 3, block + pltpu.roll(block, 5, 0) + base, 0.0)
        pos[slot] = place
        feat[slot] = jnp.where(row == 3, 1.0, place) * block[6:7]
        h, m, l = split3(flat_of(place))
        near_xy[slot] = jnp.concatenate([h, m, h, l, h, m], 0)
        if step == 0:
            rate = 1.0 / (SPREAD * (type_width + block[7:8]))
            near_type[slot] = jnp.concatenate(split3(rate), 0)
        return slot

    def flat_of(place):
        x = place[0:1] - 0.5 * bx
        y = place[1:2] - 0.5 * by
        return jnp.where(
            row == 0, x, jnp.where(row == 1, y, jnp.where(row == 2, x * x + y * y, jnp.where(row == 3, 1.0, 0.0)))
        )

    types = table.shape[1]
    type_row = lax.broadcasted_iota(jnp.int32, (types, atoms), 0)
    type_width = jnp.zeros((types, atoms), F32)
    for t in range(types):
        type_width = jnp.where(type_row == t, table[1, t] * table[1, t], type_width)

    def own_side(step):
        p = flat_of(pos[OWN])
        turned = jnp.where(
            row < 2, -2.0 * p, jnp.where(row == 2, 1.0, jnp.where(row == 3, p[2:3], 0.0))
        )
        h, m, l = split3(turned)
        rows = jnp.concatenate([h, h, m, h, l, m], 0).astype(F32)
        side_xy[...] = jnp.transpose(rows).astype(BF16)
        col_z[...] = jnp.broadcast_to(jnp.transpose(pos[OWN])[:, 2:3], (atoms, 128))
        if step == 0:
            match = jnp.where(type_row == kinds_in[0], 1.0, 0.0)
            side_type[...] = jnp.transpose(jnp.concatenate([match] * 3, 0)).astype(BF16)

    def squares(step, slot, xy, rows=slice(None)):
        xy[rows] = dot_nn(side_xy[rows], near_xy[slot])
        if step == 0:
            rates[slot - FIRST, rows] = dot_nn(side_type[rows], near_type[slot])

    tall = min(16, atoms)

    def values(start, stop, *pairs):
        for r in range(start, stop, tall):
            rows = slice(r, r + tall)
            z = col_z[rows]
            sums = [acc[f, rows] for f in range(4)]
            for slot, xy in pairs:
                for k in range(0, atoms, 128):
                    at = slice(k, k + 128)
                    dz = z - pos[slot, 2:3, at]
                    rate = rates[slot - FIRST, rows, at]
                    value = jnp.exp2((xy[rows, at] + dz * dz) * rate) * rate
                    for f in range(4):
                        sums[f] = sums[f] + value * feat[slot, f : f + 1, at]
            for f in range(4):
                acc[f, rows] = sums[f]

    def spread(a, b):
        p0 = max(0, a * bx)
        p1 = min(rx, a * bx + bx + 5)
        r0, r1 = {-1: (0, 8), 0: (0, ry), 1: (by, ry)}[b]
        slot = slot_of(a, b)
        block = pk[slot]
        charge = block[6:7]
        ax, ay = block[0:1], block[1:2]
        fx, fy, fz = block[3:4], block[4:5], block[5:6]
        ax = ax + float(a * bx)
        ay = ay + float(b * by)
        in_x = ax + 1.0 + (s * bx).astype(F32) < float(n_x)
        in_y = ay + 1.0 + (q * by).astype(F32) < float(n_y)
        ux = jnp.where(in_x, fx, 0.0)
        uy = jnp.where(in_y, fy, 0.0)
        tx = iota_f((p1 - p0, atoms), 0) + float(p0 - 2) - ax
        wx = tap_of(tx) * (1.0 - fx) + tap_of(tx - 1.0) * ux
        ty = iota_f((r1 - r0, atoms), 0) + float(r0 - 2) - ay
        wy = tap_of(ty) * (1.0 - fy) + tap_of(ty - 1.0) * uy
        low, up = charge * (1.0 - fz), charge * fz
        planes = []
        for w in (wx * low, wx * up):
            plane = jnp.concatenate([wy * w[p : p + 1] for p in range(p1 - p0)], 0)
            planes.extend(split2(plane))
        size = planes[0].shape[0]
        out = dot_nt(jnp.concatenate(planes, 0), hot[slot])
        shape = (p1 - p0, r1 - r0, gz)
        dens[p0:p1, r0:r1] += (out[:size] + out[size : 2 * size]).reshape(shape)
        dens_up[p0:p1, r0:r1] += (out[2 * size : 3 * size] + out[3 * size :]).reshape(shape)

    i = lax.broadcasted_iota(jnp.int32, (gz, gz), 0)
    j = lax.broadcasted_iota(jnp.int32, (gz, gz), 1)
    blur_z = tap_of((i - j).astype(F32)).astype(BF16)
    blur_up = tap_of((i + 1 - j).astype(F32)).astype(BF16)

    def z_blur(x, matrix):
        h, l = split2(x)
        size = x.shape[0]
        both = dot_nn(jnp.concatenate([h, l], 0), matrix)
        return both[:size] + both[size:]

    gx = lax.broadcasted_iota(jnp.int32, (rx, ry, gz), 0) - 2 + s * bx
    gy = lax.broadcasted_iota(jnp.int32, (rx, ry, gz), 1) - 2 + q * by
    inside = (gx >= 0) & (gx < n_x) & (gy >= 0) & (gy < n_y)

    def scales():
        wxp, wyp = bx + 13, by + 16
        tx = lax.broadcasted_iota(jnp.int32, (wxp, wyp, gz), 0) - 6 + s * bx
        ty = lax.broadcasted_iota(jnp.int32, (wxp, wyp, gz), 1) - 8 + q * by
        valid = (tx >= 0) & (tx < n_x) & (ty >= 0) & (ty < n_y)
        t = jnp.where(valid, wide[...], 0.0)
        box_z = band(gz, 4, False)

        def boxed(v):
            two = v[:-1] + v[1:]
            four = two[:-2] + two[2:]
            eight = four[:-4] + four[4:]
            v = eight[:rx] + v[8 : 8 + rx]
            size = wyp
            two = v + pltpu.roll(v, size - 1, 1)
            four = two + pltpu.roll(two, size - 2, 1)
            eight = four + pltpu.roll(four, size - 4, 1)
            nine = eight + pltpu.roll(v, size - 8, 1)
            v = pltpu.roll(nine, size - 2, 1)[:, :ry]
            v = v.reshape(rx * ry, gz)
            h, m, l = split3(v)
            size = v.shape[0]
            out = dot_nn(jnp.concatenate([h, m, l], 0), box_z)
            out = out[:size] + out[size : 2 * size] + out[2 * size :]
            return out.reshape(rx, ry, gz) * (1.0 / 729.0)

        mean_one = boxed(t)
        mean_two = boxed(t * t)
        inverse_scale = lax.rsqrt(mean_two - mean_one * mean_one + EPSILON)
        inv_ref[...] = jnp.where(inside, inverse_scale, 0.0)
        tgt_ref[...] = pltpu.roll(t[4 : 4 + rx], wyp - 6, 1)[:, :ry]

    def map_part():
        size = rx * ry
        blurred = z_blur(dens[...].reshape(size, gz), blur_z)
        blurred = blurred + z_blur(dens_up[...].reshape(size, gz), blur_up)
        blurred = blurred.reshape(rx, ry, gz)
        residual = (blurred - tgt_ref[...]) * inv_ref[...]
        along = TAPS[0] * (residual[0 : bx + 1] + residual[4 : bx + 5])
        along = along + TAPS[1] * (residual[1 : bx + 2] + residual[3 : bx + 4])
        along = along + TAPS[2] * residual[2 : bx + 3]
        down = TAPS[0] * along
        for k in range(1, 5):
            down = down + TAPS[k] * pltpu.roll(along, ry - k, 1)
        return z_blur(down.reshape((bx + 1) * ry, gz), blur_z).reshape(bx + 1, ry, gz)

    def gradient_of(potential):
        px = lax.broadcasted_iota(jnp.int32, (bx + 1, ry, gz), 0) + s * bx
        py = lax.broadcasted_iota(jnp.int32, (bx + 1, ry, gz), 1) + q * by
        py_local = lax.broadcasted_iota(jnp.int32, (bx + 1, ry, gz), 1)
        field = jnp.where((px < n_x) & (py < n_y) & (py_local <= by), potential, 0.0)
        own = pk[OWN]
        ax, ay = own[0:1], own[1:2]
        fx, fy, fz = own[3:4], own[4:5], own[5:6]
        size = (bx + 1) * ry
        field = field.reshape(size, gz)
        up = pltpu.roll(field, gz - 1, 1)
        out = dot_nn(jnp.concatenate(split2(field) + split2(up), 0), hot[OWN])
        at_low = out[:size] + out[size : 2 * size]
        slope = out[2 * size : 3 * size] + out[3 * size :] - at_low
        value = at_low + fz * slope
        iy = iota_f((ry, atoms), 0)
        low_y = jnp.where(iy == ay, 1.0, 0.0)
        up_y = jnp.where(iy == ay + 1.0, 1.0, 0.0)
        wy = low_y * (1.0 - fy) + up_y * fy
        sy = up_y - low_y
        grad_x = jnp.zeros((1, atoms), F32)
        grad_y = jnp.zeros((1, atoms), F32)
        grad_z = jnp.zeros((1, atoms), F32)
        for p in range(bx + 1):
            low_x = jnp.where(ax == float(p), 1.0, 0.0)
            up_x = jnp.where(ax + 1.0 == float(p), 1.0, 0.0)
            wx = low_x * (1.0 - fx) + up_x * fx
            sx = up_x - low_x
            v = value[p * ry : (p + 1) * ry]
            g = slope[p * ry : (p + 1) * ry]
            grad_x = grad_x + sx * jnp.sum(wy * v, 0, keepdims=True)
            grad_y = grad_y + wx * jnp.sum(sy * v, 0, keepdims=True)
            grad_z = grad_z + wx * jnp.sum(wy * g, 0, keepdims=True)
        return own[6:7] * jnp.concatenate([grad_x, grad_y, grad_z], 0)

    for step in range(steps):
        last = step == steps - 1
        group = 0 if step == 0 else step + 1
        source, landing = (packet, packets) if step == 0 else (now, later)
        load_near(step, 0, 0)
        own_side(step)
        acc[...] = jnp.zeros_like(acc)
        dens[...] = jnp.zeros_like(dens)
        dens_up[...] = jnp.zeros_like(dens_up)
        squares(step, OWN, xy0)
        values(0, atoms, (OWN, xy0))
        spread(0, 0)

        def two_cells(k, carry):
            da = jnp.minimum(k, 1)
            db = jnp.where(k == 1, 0, jnp.where(k == 3, -1, 1))
            each([(-da, -db), (da, db)], lambda a, b: packet_copy(source, landing, group, a, b, False).wait_recv())

            if step == 0:

                @pl.when(k == 0)
                def _():
                    each(others, lambda a, b: target_copy(a, b, True).start())

            one = load_near(step, -da, -db)
            two = load_near(step, da, db)
            for h in range(0, atoms, 64):
                part = slice(h, h + 64)
                squares(step, one, xy0, part)
                squares(step, two, xy1, part)
                if h > 0:
                    values(h - 64, h, (one, xy0), (two, xy1))
            values(atoms - 64, atoms, (one, xy0), (two, xy1))
            return carry

        lax.fori_loop(0, len(near) // 2, two_cells, 0)
        each(far, lambda a, b: packet_copy(source, landing, group, a, b, False).wait_recv())
        for a, b in far:
            load_cell(step, a, b)
        for a, b in others:
            spread(a, b)
        if step == 0:
            each(others, lambda a, b: target_copy(a, b, False).wait_recv())
            scales()
        potential = map_part()
        if last:
            pot[...] = potential[:bx, :by]
        gradient = gradient_of(potential)
        lane = lax.broadcasted_iota(jnp.int32, (atoms, 128), 1)
        turned = jnp.zeros((atoms, 128), F32)
        for f in range(4):
            turned = jnp.where(lane == f, jnp.sum(acc[f], 1, keepdims=True), turned)
        sums = jnp.transpose(turned)[0:8]
        here = pos[OWN][0:3]
        pair = (SPREAD * pk[OWN][6:7]) * (here * sums[3:4] - sums[0:3])
        new_velocity = vel[...] + TIME_STEP * (pair - gradient) / mass[...]
        new_moved = moved[...] + TIME_STEP * new_velocity
        if last:
            vel_out[...] = new_velocity
            moved_out[...] = new_moved
        else:
            vel[...] = new_velocity
            moved[...] = new_moved
            now[...] = pk[OWN][3:6] + TIME_STEP * new_velocity
            each(others, lambda a, b: packet_copy(now, later, step + 2, a, b, True).start())

    each(others, lambda a, b: packet_copy(packet, packets, 0, a, b, True).wait_send())
    each(others, lambda a, b: target_copy(a, b, True).wait_send())
    for step in range(1, steps):
        each(others, lambda a, b: packet_copy(now, later, step + 1, a, b, True).wait_send())


STEPS = 2


def finish(counts, vel, moved, pot, vel_out, moved_out, pot_out):
    live = lax.broadcasted_iota(jnp.int32, vel.shape, 1) < counts[0, 0]
    vel_out[:, 0, 0, :] = jnp.where(live, vel[...], 0.0)
    moved_out[:, 0, 0, :] = jnp.where(live, moved[...], 0.0)
    pot_out[...] = pot[...]


def in_hbm(x):
    return pltpu.with_memory_space_constraint(x, pltpu.HBM)


def per_device(fraction, velocity, anchor, atom_types, counts, type_table, target):
    atoms = fraction.shape[3]
    bx, by, gz = target.shape
    types = type_table.shape[1]
    n_x = bx * lax.axis_size("cells")
    n_y = by * lax.axis_size("grp")
    row = jax.ShapeDtypeStruct((3, atoms), F32)
    final = jax.ShapeDtypeStruct(velocity.shape, F32)
    field = jax.ShapeDtypeStruct((bx, by, gz), F32)
    region = pltpu.VMEM((bx + 5, by + 8, gz), F32)
    three = pltpu.VMEM((3, atoms), F32)
    square = pltpu.VMEM((atoms, atoms), F32)
    done = pl.pallas_call(
        functools.partial(kernel, STEPS, bx, by, gz, n_x, n_y),
        out_shape=[row, row, field],
        in_specs=[HBM, HBM, HBM, HBM, SMEM, HBM, HBM],
        out_specs=[VMEM] * 3,
        scratch_shapes=[
            pltpu.VMEM(fraction.shape, F32),
            pltpu.VMEM(velocity.shape, F32),
            pltpu.VMEM(anchor.shape, jnp.int32),
            pltpu.VMEM(atom_types.shape, jnp.int32),
            pltpu.SMEM(type_table.shape, F32),
            pltpu.VMEM((8, atoms), F32),
            pltpu.VMEM((1, atoms), F32),
            pltpu.VMEM((SLOTS, 8, atoms), F32),
            pltpu.VMEM((bx + 13, by + 16, gz), F32),
            three,
            pltpu.VMEM((SLOTS, 3, atoms), F32),
            three,
            three,
            pltpu.VMEM((SLOTS, 8, atoms), F32),
            pltpu.VMEM((SLOTS, 8, atoms), F32),
            pltpu.VMEM((SLOTS, 8, atoms), F32),
            pltpu.VMEM((SLOTS, gz, atoms), BF16),
            pltpu.VMEM((atoms, 48), BF16),
            pltpu.VMEM((atoms, 3 * types), BF16),
            pltpu.VMEM((SLOTS, 48, atoms), BF16),
            pltpu.VMEM((SLOTS, 3 * types, atoms), BF16),
            pltpu.VMEM((atoms, 128), F32),
            square,
            square,
            pltpu.VMEM((3 * NB, atoms, atoms), F32),
            pltpu.VMEM((4, atoms, 128), F32),
            region,
            region,
            region,
            region,
            pltpu.SemaphoreType.DMA((STEPS + 1, SLOTS)),
            pltpu.SemaphoreType.DMA((STEPS + 1, SLOTS)),
            pltpu.SemaphoreType.DMA((6,)),
        ],
        compiler_params=pltpu.CompilerParams(
            collective_id=0, has_side_effects=True, vmem_limit_bytes=40 * 2**20
        ),
        name="dynamics",
    )(*map(in_hbm, (fraction, velocity, anchor, atom_types)), counts, in_hbm(type_table), in_hbm(target))
    return tuple(
        pl.pallas_call(
            finish,
            out_shape=[final, final, field],
            in_specs=[SMEM, VMEM, VMEM, VMEM],
            out_specs=[VMEM] * 3,
            compiler_params=pltpu.CompilerParams(vmem_limit_bytes=4 * 2**20),
            name="finish",
        )(counts, *done)
    )


def solution(mesh):
    placed = (
        P(None, "cells", "grp", None),
        P(None, "cells", "grp", None),
        P(None, "cells", "grp", None),
        P("cells", "grp", None),
        P("cells", "grp"),
        P(),
        P("cells", "grp", None),
    )
    return jax.shard_map(
        per_device,
        mesh=mesh,
        in_specs=placed,
        out_specs=(
            P(None, "cells", "grp", None),
            P(None, "cells", "grp", None),
            P("cells", "grp", None),
        ),
        check_vma=False,
    )
```

```python
import functools
import math

import jax
import jax.numpy as jnp
from jax import lax
from jax.experimental import pallas as pl
from jax.experimental.pallas import tpu as pltpu
from jax.sharding import PartitionSpec as P

EPSILON = 1e-06
TIME_STEP = 0.5
TAPS = (1.0 / 16.0, 4.0 / 16.0, 6.0 / 16.0, 4.0 / 16.0, 1.0 / 16.0)
F32 = jnp.float32
BF16 = jnp.bfloat16
RX, RY = 2, 1
NB = 2 * RY + 1
SLOTS = (2 * RX + 1) * NB
OWN = RX * NB + RY
MESH = pl.DeviceIdType.MESH
VMEM = pl.BlockSpec(memory_space=pltpu.VMEM)
SMEM = pl.BlockSpec(memory_space=pltpu.SMEM)
HBM = pl.BlockSpec(memory_space=pltpu.HBM)
NEIGHBOURS = tuple(
    (a, b) for a in range(-RX, RX + 1) for b in range(-RY, RY + 1) if (a, b) != (0, 0)
)


def slot_of(a, b):
    return (a + RX) * NB + (b + RY)


def exists(a, b):
    s = lax.axis_index("cells") + a
    q = lax.axis_index("grp") + b
    ns, nq = lax.axis_size("cells"), lax.axis_size("grp")
    return (s >= 0) & (s < ns) & (q >= 0) & (q < nq)


def target_piece(a, b, bx, by):
    x0 = max(0, -6 - a * bx)
    x1 = min(bx, bx + 7 - a * bx)
    y0, y1 = {-1: (by - 8, by), 0: (0, by), 1: (0, 8)}[b]
    return x0, x1, y0, y1


def split2(x):
    hi = x.astype(BF16)
    return hi, (x - hi.astype(F32)).astype(BF16)


def split3(x):
    hi = x.astype(BF16)
    rest = x - hi.astype(F32)
    mid = rest.astype(BF16)
    return hi, mid, (rest - mid.astype(F32)).astype(BF16)


def dot_nn(x, y):
    return lax.dot_general(x, y, (((1,), (0,)), ((), ())), preferred_element_type=F32)


def dot_nt(x, y):
    return lax.dot_general(x, y, (((1,), (1,)), ((), ())), preferred_element_type=F32)


def iota_f(shape, dim):
    return lax.broadcasted_iota(jnp.int32, shape, dim).astype(F32)


def tap_of(t):
    u = jnp.abs(t)
    return jnp.where(
        u == 0.0, TAPS[2], jnp.where(u == 1.0, TAPS[1], jnp.where(u == 2.0, TAPS[0], 0.0))
    )


def band(gz, radius, taps):
    i = lax.broadcasted_iota(jnp.int32, (gz, gz), 0)
    j = lax.broadcasted_iota(jnp.int32, (gz, gz), 1)
    t = (i - j).astype(F32)
    if taps:
        return tap_of(t).astype(BF16)
    return jnp.where(jnp.abs(t) <= radius, 1.0, 0.0).astype(BF16)


def pack(fraction, anchor, kinds, counts, table, packet, mass):
    atoms = packet.shape[1]
    n = counts[0, 0]
    kind = kinds[0]
    lane = lax.broadcasted_iota(jnp.int32, (1, atoms), 1)
    rows = []
    for r in range(3):
        row = jnp.zeros((1, atoms), F32)
        for t in range(table.shape[1]):
            row = jnp.where(kind == t, table[r, t], row)
        rows.append(row)
    packet[0:3] = anchor[:, 0, 0, :].astype(F32)
    packet[3:6] = fraction[:, 0, 0, :]
    packet[6:7] = jnp.where(lane < n, rows[0], 0.0)
    packet[7:8] = rows[1] * rows[1]
    mass[...] = rows[2]


SPREAD = -2.0 / math.log2(math.e)
FIRST = NB * (RX - 1)


def kernel(steps, bx, by, gz, n_x, n_y, *refs):
    (fraction, velocity, anchor, kinds, own_counts, table_hbm, target,
     vel_out, moved_out, pot,
     fraction_in, velocity_in, anchor_in, kinds_in, table, packet, mass, packets, wide, now, later, vel, moved,
     pk, pos, feat, hot, side_xy, side_type, near_xy, near_type, col_z, xy0, xy1, rates,
     acc, taps_x, taps_y, dens, dens_up, inv_ref, tgt_ref,
     send_sem, recv_sem, load_sem) = refs
    atoms = packet.shape[1]
    s, q = lax.axis_index("cells"), lax.axis_index("grp")
    rx, ry = bx + 5, by + 8
    near = [(0, -1), (0, 1), (-1, 0), (1, 0), (-1, -1), (1, 1), (-1, 1), (1, -1)]
    far = [(a, b) for a, b in NEIGHBOURS if abs(a) > 1]
    others = near + far

    barrier = pltpu.get_barrier_semaphore()
    total = jnp.int32(0)
    for a, b in NEIGHBOURS:
        there = exists(a, b)
        total = total + there.astype(jnp.int32)

        @pl.when(there)
        def _(a=a, b=b):
            pl.semaphore_signal(barrier, inc=1, device_id=(s + a, q + b), device_id_type=MESH)

    own_target = wide.at[6 : 6 + bx, 8 : 8 + by]
    loads = [
        pltpu.make_async_copy(src, dst, load_sem.at[k])
        for k, (src, dst) in enumerate(
            [(anchor, anchor_in), (fraction, fraction_in), (kinds, kinds_in), (table_hbm, table),
             (velocity, velocity_in), (target, own_target)]
        )
    ]
    for load in loads:
        load.start()
    for load in loads[:4]:
        load.wait()
    pack(fraction_in, anchor_in, kinds_in, own_counts, table, packet, mass)
    pl.semaphore_wait(barrier, total)

    def packet_copy(src, dst, group, a, b, there):
        mine, back = slot_of(a, b), slot_of(-a, -b)
        slot = back if there else mine
        return pltpu.make_async_remote_copy(
            src_ref=src,
            dst_ref=dst.at[slot],
            send_sem=send_sem.at[group, mine],
            recv_sem=recv_sem.at[group, slot],
            device_id=(s + a, q + b),
            device_id_type=MESH,
        )

    def target_copy(a, b, there):
        mine, back = slot_of(a, b), slot_of(-a, -b)
        slot = back if there else mine
        c, d = (-a, -b) if there else (a, b)
        x0, x1, y0, y1 = target_piece(c, d, bx, by)
        X, Y = 6 + c * bx + x0, 8 + d * by + y0
        return pltpu.make_async_remote_copy(
            src_ref=target.at[x0:x1, y0:y1],
            dst_ref=wide.at[X : X + x1 - x0, Y : Y + y1 - y0],
            send_sem=send_sem.at[1, mine],
            recv_sem=recv_sem.at[1, slot],
            device_id=(s + a, q + b),
            device_id_type=MESH,
        )

    def each(cells, act):
        for a, b in cells:

            @pl.when(exists(a, b))
            def _(a=a, b=b):
                act(a, b)

    each(others, lambda a, b: packet_copy(packet, packets, 0, a, b, True).start())
    for load in loads[4:]:
        load.wait()
    vel[...] = velocity_in[:, 0, 0, :]
    moved[...] = jnp.zeros_like(moved)

    row = lax.broadcasted_iota(jnp.int32, (8, atoms), 0)
    iz = iota_f((gz, atoms), 0).astype(BF16)

    def load_cell(step, a, b):
        slot = slot_of(a, b)
        own = isinstance(slot, int) and slot == OWN
        if step == 0:
            block = packet[...] if own else packets[slot]
            if not own:
                block = jnp.where(exists(a, b), block, 0.0)
            hot[slot] = jnp.where(
                iz == block[2:3].astype(BF16), jnp.ones((), BF16), jnp.zeros((), BF16)
            )
        else:
            block = pk[slot]
            fresh = now[...] if own else jnp.where(exists(a, b), later[slot], 0.0)
            block = jnp.concatenate([block[0:3], fresh, block[6:8]], 0)
        pk[slot] = block
        return slot, block

    def load_near(step, a, b):
        slot, block = load_cell(step, a, b)
        base_x = jnp.asarray(a * bx, F32)
        base_y = jnp.asarray(b * by, F32)
        base = jnp.where(row == 0, base_x, jnp.where(row == 1, base_y, 0.0))
        place = jnp.where(row < 3, block + pltpu.roll(block, 5, 0) + base, 0.0)
        pos[slot] = place
        feat[slot] = jnp.where(row == 3, 1.0, place) * block[6:7]
        h, m, l = split3(flat_of(place))
        near_xy[slot] = jnp.concatenate([h, m, h, l, h, m], 0)
        if step == 0:
            rate = 1.0 / (SPREAD * (type_width + block[7:8]))
            near_type[slot] = jnp.concatenate(split3(rate), 0)
        return slot

    def flat_of(place):
        x = place[0:1] - 0.5 * bx
        y = place[1:2] - 0.5 * by
        return jnp.where(
            row == 0, x, jnp.where(row == 1, y, jnp.where(row == 2, x * x + y * y, jnp.where(row == 3, 1.0, 0.0)))
        )

    types = table.shape[1]
    type_row = lax.broadcasted_iota(jnp.int32, (types, atoms), 0)
    type_width = jnp.zeros((types, atoms), F32)
    for t in range(types):
        type_width = jnp.where(type_row == t, table[1, t] * table[1, t], type_width)

    def own_side(step):
        p = flat_of(pos[OWN])
        turned = jnp.where(
            row < 2, -2.0 * p, jnp.where(row == 2, 1.0, jnp.where(row == 3, p[2:3], 0.0))
        )
        h, m, l = split3(turned)
        rows = jnp.concatenate([h, h, m, h, l, m], 0).astype(F32)
        side_xy[...] = jnp.transpose(rows).astype(BF16)
        col_z[...] = jnp.broadcast_to(jnp.transpose(pos[OWN])[:, 2:3], (atoms, 128))
        if step == 0:
            match = jnp.where(type_row == kinds_in[0], 1.0, 0.0)
            side_type[...] = jnp.transpose(jnp.concatenate([match] * 3, 0)).astype(BF16)

    def squares(step, slot, xy, rows=slice(None)):
        xy[rows] = dot_nn(side_xy[rows], near_xy[slot])
        if step == 0:
            rates[slot - FIRST, rows] = dot_nn(side_type[rows], near_type[slot])

    tall = min(16, atoms)

    def values(start, stop, *pairs):
        for r in range(start, stop, tall):
            rows = slice(r, r + tall)
            z = col_z[rows]
            sums = [acc[f, rows] for f in range(4)]
            for slot, xy in pairs:
                for k in range(0, atoms, 128):
                    at = slice(k, k + 128)
                    dz = z - pos[slot, 2:3, at]
                    rate = rates[slot - FIRST, rows, at]
                    value = jnp.exp2((xy[rows, at] + dz * dz) * rate) * rate
                    for f in range(4):
                        sums[f] = sums[f] + value * feat[slot, f : f + 1, at]
            for f in range(4):
                acc[f, rows] = sums[f]

    def spread(step, a, b):
        p0 = max(0, a * bx)
        p1 = min(rx, a * bx + bx + 5)
        r0, r1 = {-1: (0, 8), 0: (0, ry), 1: (by, ry)}[b]
        slot = slot_of(a, b)
        block = pk[slot]
        charge = block[6:7]
        ax, ay = block[0:1], block[1:2]
        fx, fy, fz = block[3:4], block[4:5], block[5:6]
        xs, ys = slice(0, p1 - p0), slice(0, r1 - r0)
        if step == 0:
            ax = ax + float(a * bx)
            ay = ay + float(b * by)
            in_x = ax + 1.0 + (s * bx).astype(F32) < float(n_x)
            in_y = ay + 1.0 + (q * by).astype(F32) < float(n_y)
            tx = iota_f((p1 - p0, atoms), 0) + float(p0 - 2) - ax
            ty = iota_f((r1 - r0, atoms), 0) + float(r0 - 2) - ay
            taps_x[slot, 0, xs] = tap_of(tx)
            taps_x[slot, 1, xs] = jnp.where(in_x, tap_of(tx - 1.0), 0.0)
            taps_y[slot, 0, ys] = tap_of(ty)
            taps_y[slot, 1, ys] = jnp.where(in_y, tap_of(ty - 1.0), 0.0)
        wx = taps_x[slot, 0, xs] * (1.0 - fx) + taps_x[slot, 1, xs] * fx
        wy = taps_y[slot, 0, ys] * (1.0 - fy) + taps_y[slot, 1, ys] * fy
        low, up = charge * (1.0 - fz), charge * fz
        planes = []
        for w in (wx * low, wx * up):
            plane = jnp.concatenate([wy * w[p : p + 1] for p in range(p1 - p0)], 0)
            planes.extend(split2(plane))
        size = planes[0].shape[0]
        out = dot_nt(jnp.concatenate(planes, 0), hot[slot])
        shape = (p1 - p0, r1 - r0, gz)
        dens[p0:p1, r0:r1] += (out[:size] + out[size : 2 * size]).reshape(shape)
        dens_up[p0:p1, r0:r1] += (out[2 * size : 3 * size] + out[3 * size :]).reshape(shape)

    i = lax.broadcasted_iota(jnp.int32, (gz, gz), 0)
    j = lax.broadcasted_iota(jnp.int32, (gz, gz), 1)
    blur_z = tap_of((i - j).astype(F32)).astype(BF16)
    blur_up = tap_of((i + 1 - j).astype(F32)).astype(BF16)

    def z_blur(x, matrix):
        h, l = split2(x)
        size = x.shape[0]
        both = dot_nn(jnp.concatenate([h, l], 0), matrix)
        return both[:size] + both[size:]

    gx = lax.broadcasted_iota(jnp.int32, (rx, ry, gz), 0) - 2 + s * bx
    gy = lax.broadcasted_iota(jnp.int32, (rx, ry, gz), 1) - 2 + q * by
    inside = (gx >= 0) & (gx < n_x) & (gy >= 0) & (gy < n_y)

    def scales():
        wxp, wyp = bx + 13, by + 16
        tx = lax.broadcasted_iota(jnp.int32, (wxp, wyp, gz), 0) - 6 + s * bx
        ty = lax.broadcasted_iota(jnp.int32, (wxp, wyp, gz), 1) - 8 + q * by
        valid = (tx >= 0) & (tx < n_x) & (ty >= 0) & (ty < n_y)
        t = jnp.where(valid, wide[...], 0.0)
        box_z = band(gz, 4, False)

        def boxed(v):
            two = v[:-1] + v[1:]
            four = two[:-2] + two[2:]
            eight = four[:-4] + four[4:]
            v = eight[:rx] + v[8 : 8 + rx]
            size = wyp
            two = v + pltpu.roll(v, size - 1, 1)
            four = two + pltpu.roll(two, size - 2, 1)
            eight = four + pltpu.roll(four, size - 4, 1)
            nine = eight + pltpu.roll(v, size - 8, 1)
            v = pltpu.roll(nine, size - 2, 1)[:, :ry]
            v = v.reshape(rx * ry, gz)
            h, m, l = split3(v)
            size = v.shape[0]
            out = dot_nn(jnp.concatenate([h, m, l], 0), box_z)
            out = out[:size] + out[size : 2 * size] + out[2 * size :]
            return out.reshape(rx, ry, gz) * (1.0 / 729.0)

        mean_one = boxed(t)
        mean_two = boxed(t * t)
        inverse_scale = lax.rsqrt(mean_two - mean_one * mean_one + EPSILON)
        inv_ref[...] = jnp.where(inside, inverse_scale, 0.0)
        tgt_ref[...] = pltpu.roll(t[4 : 4 + rx], wyp - 6, 1)[:, :ry]

    def map_part():
        size = rx * ry
        blurred = z_blur(dens[...].reshape(size, gz), blur_z)
        blurred = blurred + z_blur(dens_up[...].reshape(size, gz), blur_up)
        blurred = blurred.reshape(rx, ry, gz)
        residual = (blurred - tgt_ref[...]) * inv_ref[...]
        along = TAPS[0] * (residual[0 : bx + 1] + residual[4 : bx + 5])
        along = along + TAPS[1] * (residual[1 : bx + 2] + residual[3 : bx + 4])
        along = along + TAPS[2] * residual[2 : bx + 3]
        down = TAPS[0] * along
        for k in range(1, 5):
            down = down + TAPS[k] * pltpu.roll(along, ry - k, 1)
        return z_blur(down.reshape((bx + 1) * ry, gz), blur_z).reshape(bx + 1, ry, gz)

    def gradient_of(potential):
        px = lax.broadcasted_iota(jnp.int32, (bx + 1, ry, gz), 0) + s * bx
        py = lax.broadcasted_iota(jnp.int32, (bx + 1, ry, gz), 1) + q * by
        py_local = lax.broadcasted_iota(jnp.int32, (bx + 1, ry, gz), 1)
        field = jnp.where((px < n_x) & (py < n_y) & (py_local <= by), potential, 0.0)
        own = pk[OWN]
        ax, ay = own[0:1], own[1:2]
        fx, fy, fz = own[3:4], own[4:5], own[5:6]
        size = (bx + 1) * ry
        field = field.reshape(size, gz)
        up = pltpu.roll(field, gz - 1, 1)
        out = dot_nn(jnp.concatenate(split2(field) + split2(up), 0), hot[OWN])
        at_low = out[:size] + out[size : 2 * size]
        slope = out[2 * size : 3 * size] + out[3 * size :] - at_low
        value = at_low + fz * slope
        iy = iota_f((ry, atoms), 0)
        low_y = jnp.where(iy == ay, 1.0, 0.0)
        up_y = jnp.where(iy == ay + 1.0, 1.0, 0.0)
        wy = low_y * (1.0 - fy) + up_y * fy
        sy = up_y - low_y
        grad_x = jnp.zeros((1, atoms), F32)
        grad_y = jnp.zeros((1, atoms), F32)
        grad_z = jnp.zeros((1, atoms), F32)
        for p in range(bx + 1):
            low_x = jnp.where(ax == float(p), 1.0, 0.0)
            up_x = jnp.where(ax + 1.0 == float(p), 1.0, 0.0)
            wx = low_x * (1.0 - fx) + up_x * fx
            sx = up_x - low_x
            v = value[p * ry : (p + 1) * ry]
            g = slope[p * ry : (p + 1) * ry]
            grad_x = grad_x + sx * jnp.sum(wy * v, 0, keepdims=True)
            grad_y = grad_y + wx * jnp.sum(sy * v, 0, keepdims=True)
            grad_z = grad_z + wx * jnp.sum(wy * g, 0, keepdims=True)
        return own[6:7] * jnp.concatenate([grad_x, grad_y, grad_z], 0)

    for step in range(steps):
        last = step == steps - 1
        group = 0 if step == 0 else step + 1
        source, landing = (packet, packets) if step == 0 else (now, later)
        load_near(step, 0, 0)
        own_side(step)
        acc[...] = jnp.zeros_like(acc)
        dens[...] = jnp.zeros_like(dens)
        dens_up[...] = jnp.zeros_like(dens_up)
        squares(step, OWN, xy0)
        values(0, atoms, (OWN, xy0))
        spread(step, 0, 0)

        def two_cells(k, carry):
            da = jnp.minimum(k, 1)
            db = jnp.where(k == 1, 0, jnp.where(k == 3, -1, 1))
            each([(-da, -db), (da, db)], lambda a, b: packet_copy(source, landing, group, a, b, False).wait_recv())

            if step == 0:

                @pl.when(k == 0)
                def _():
                    each(others, lambda a, b: target_copy(a, b, True).start())

            one = load_near(step, -da, -db)
            two = load_near(step, da, db)
            for h in range(0, atoms, 64):
                part = slice(h, h + 64)
                squares(step, one, xy0, part)
                squares(step, two, xy1, part)
                if h > 0:
                    values(h - 64, h, (one, xy0), (two, xy1))
            values(atoms - 64, atoms, (one, xy0), (two, xy1))
            return carry

        lax.fori_loop(0, len(near) // 2, two_cells, 0)
        each(far, lambda a, b: packet_copy(source, landing, group, a, b, False).wait_recv())
        for a, b in far:
            load_cell(step, a, b)
        for a, b in others:
            spread(step, a, b)
        if step == 0:
            each(others, lambda a, b: target_copy(a, b, False).wait_recv())
            scales()
        potential = map_part()
        if last:
            pot[...] = potential[:bx, :by]
        gradient = gradient_of(potential)
        lane = lax.broadcasted_iota(jnp.int32, (atoms, 128), 1)
        turned = jnp.zeros((atoms, 128), F32)
        for f in range(4):
            turned = jnp.where(lane == f, jnp.sum(acc[f], 1, keepdims=True), turned)
        sums = jnp.transpose(turned)[0:8]
        here = pos[OWN][0:3]
        pair = (SPREAD * pk[OWN][6:7]) * (here * sums[3:4] - sums[0:3])
        new_velocity = vel[...] + TIME_STEP * (pair - gradient) / mass[...]
        new_moved = moved[...] + TIME_STEP * new_velocity
        if last:
            vel_out[...] = new_velocity
            moved_out[...] = new_moved
        else:
            vel[...] = new_velocity
            moved[...] = new_moved
            now[...] = pk[OWN][3:6] + TIME_STEP * new_velocity
            each(others, lambda a, b: packet_copy(now, later, step + 2, a, b, True).start())

    each(others, lambda a, b: packet_copy(packet, packets, 0, a, b, True).wait_send())
    each(others, lambda a, b: target_copy(a, b, True).wait_send())
    for step in range(1, steps):
        each(others, lambda a, b: packet_copy(now, later, step + 1, a, b, True).wait_send())


STEPS = 2


def finish(counts, vel, moved, pot, vel_out, moved_out, pot_out):
    live = lax.broadcasted_iota(jnp.int32, vel.shape, 1) < counts[0, 0]
    vel_out[:, 0, 0, :] = jnp.where(live, vel[...], 0.0)
    moved_out[:, 0, 0, :] = jnp.where(live, moved[...], 0.0)
    pot_out[...] = pot[...]


def in_hbm(x):
    return pltpu.with_memory_space_constraint(x, pltpu.HBM)


def per_device(fraction, velocity, anchor, atom_types, counts, type_table, target):
    atoms = fraction.shape[3]
    bx, by, gz = target.shape
    types = type_table.shape[1]
    n_x = bx * lax.axis_size("cells")
    n_y = by * lax.axis_size("grp")
    row = jax.ShapeDtypeStruct((3, atoms), F32)
    final = jax.ShapeDtypeStruct(velocity.shape, F32)
    field = jax.ShapeDtypeStruct((bx, by, gz), F32)
    region = pltpu.VMEM((bx + 5, by + 8, gz), F32)
    three = pltpu.VMEM((3, atoms), F32)
    square = pltpu.VMEM((atoms, atoms), F32)
    done = pl.pallas_call(
        functools.partial(kernel, STEPS, bx, by, gz, n_x, n_y),
        out_shape=[row, row, field],
        in_specs=[HBM, HBM, HBM, HBM, SMEM, HBM, HBM],
        out_specs=[VMEM] * 3,
        scratch_shapes=[
            pltpu.VMEM(fraction.shape, F32),
            pltpu.VMEM(velocity.shape, F32),
            pltpu.VMEM(anchor.shape, jnp.int32),
            pltpu.VMEM(atom_types.shape, jnp.int32),
            pltpu.SMEM(type_table.shape, F32),
            pltpu.VMEM((8, atoms), F32),
            pltpu.VMEM((1, atoms), F32),
            pltpu.VMEM((SLOTS, 8, atoms), F32),
            pltpu.VMEM((bx + 13, by + 16, gz), F32),
            three,
            pltpu.VMEM((SLOTS, 3, atoms), F32),
            three,
            three,
            pltpu.VMEM((SLOTS, 8, atoms), F32),
            pltpu.VMEM((SLOTS, 8, atoms), F32),
            pltpu.VMEM((SLOTS, 8, atoms), F32),
            pltpu.VMEM((SLOTS, gz, atoms), BF16),
            pltpu.VMEM((atoms, 48), BF16),
            pltpu.VMEM((atoms, 3 * types), BF16),
            pltpu.VMEM((SLOTS, 48, atoms), BF16),
            pltpu.VMEM((SLOTS, 3 * types, atoms), BF16),
            pltpu.VMEM((atoms, 128), F32),
            square,
            square,
            pltpu.VMEM((3 * NB, atoms, atoms), F32),
            pltpu.VMEM((4, atoms, 128), F32),
            pltpu.VMEM((SLOTS, 2, bx + 5, atoms), F32),
            pltpu.VMEM((SLOTS, 2, by + 8, atoms), F32),
            region,
            region,
            region,
            region,
            pltpu.SemaphoreType.DMA((STEPS + 1, SLOTS)),
            pltpu.SemaphoreType.DMA((STEPS + 1, SLOTS)),
            pltpu.SemaphoreType.DMA((6,)),
        ],
        compiler_params=pltpu.CompilerParams(
            collective_id=0, has_side_effects=True, vmem_limit_bytes=40 * 2**20
        ),
        name="dynamics",
    )(*map(in_hbm, (fraction, velocity, anchor, atom_types)), counts, in_hbm(type_table), in_hbm(target))
    return tuple(
        pl.pallas_call(
            finish,
            out_shape=[final, final, field],
            in_specs=[SMEM, VMEM, VMEM, VMEM],
            out_specs=[VMEM] * 3,
            compiler_params=pltpu.CompilerParams(vmem_limit_bytes=4 * 2**20),
            name="finish",
        )(counts, *done)
    )


def solution(mesh):
    placed = (
        P(None, "cells", "grp", None),
        P(None, "cells", "grp", None),
        P(None, "cells", "grp", None),
        P("cells", "grp", None),
        P("cells", "grp"),
        P(),
        P("cells", "grp", None),
    )
    return jax.shard_map(
        per_device,
        mesh=mesh,
        in_specs=placed,
        out_specs=(
            P(None, "cells", "grp", None),
            P(None, "cells", "grp", None),
            P("cells", "grp", None),
        ),
        check_vma=False,
    )
```

```python
import functools
import math

import jax
import jax.numpy as jnp
from jax import lax
from jax.experimental import pallas as pl
from jax.experimental.pallas import tpu as pltpu
from jax.sharding import PartitionSpec as P

EPSILON = 1e-06
TIME_STEP = 0.5
TAPS = (1.0 / 16.0, 4.0 / 16.0, 6.0 / 16.0, 4.0 / 16.0, 1.0 / 16.0)
F32 = jnp.float32
BF16 = jnp.bfloat16
RX, RY = 2, 1
NB = 2 * RY + 1
SLOTS = (2 * RX + 1) * NB
OWN = RX * NB + RY
MESH = pl.DeviceIdType.MESH
VMEM = pl.BlockSpec(memory_space=pltpu.VMEM)
SMEM = pl.BlockSpec(memory_space=pltpu.SMEM)
HBM = pl.BlockSpec(memory_space=pltpu.HBM)
NEIGHBOURS = tuple(
    (a, b) for a in range(-RX, RX + 1) for b in range(-RY, RY + 1) if (a, b) != (0, 0)
)


def slot_of(a, b):
    return (a + RX) * NB + (b + RY)


def exists(a, b):
    s = lax.axis_index("cells") + a
    q = lax.axis_index("grp") + b
    ns, nq = lax.axis_size("cells"), lax.axis_size("grp")
    return (s >= 0) & (s < ns) & (q >= 0) & (q < nq)


def target_piece(a, b, bx, by):
    x0 = max(0, -6 - a * bx)
    x1 = min(bx, bx + 7 - a * bx)
    y0, y1 = {-1: (by - 8, by), 0: (0, by), 1: (0, 8)}[b]
    return x0, x1, y0, y1


def split2(x):
    hi = x.astype(BF16)
    return hi, (x - hi.astype(F32)).astype(BF16)


def split3(x):
    hi = x.astype(BF16)
    rest = x - hi.astype(F32)
    mid = rest.astype(BF16)
    return hi, mid, (rest - mid.astype(F32)).astype(BF16)


def dot_nn(x, y):
    return lax.dot_general(x, y, (((1,), (0,)), ((), ())), preferred_element_type=F32)


def dot_nt(x, y):
    return lax.dot_general(x, y, (((1,), (1,)), ((), ())), preferred_element_type=F32)


def iota_f(shape, dim):
    return lax.broadcasted_iota(jnp.int32, shape, dim).astype(F32)


def tap_of(t):
    u = jnp.abs(t)
    return jnp.where(
        u == 0.0, TAPS[2], jnp.where(u == 1.0, TAPS[1], jnp.where(u == 2.0, TAPS[0], 0.0))
    )


def band(gz, radius, taps):
    i = lax.broadcasted_iota(jnp.int32, (gz, gz), 0)
    j = lax.broadcasted_iota(jnp.int32, (gz, gz), 1)
    t = (i - j).astype(F32)
    if taps:
        return tap_of(t).astype(BF16)
    return jnp.where(jnp.abs(t) <= radius, 1.0, 0.0).astype(BF16)


def pack(fraction, anchor, kinds, counts, table, packet, mass):
    atoms = packet.shape[1]
    n = counts[0, 0]
    kind = kinds[0]
    lane = lax.broadcasted_iota(jnp.int32, (1, atoms), 1)
    rows = []
    for r in range(3):
        row = jnp.zeros((1, atoms), F32)
        for t in range(table.shape[1]):
            row = jnp.where(kind == t, table[r, t], row)
        rows.append(row)
    packet[0:3] = anchor[:, 0, 0, :].astype(F32)
    packet[3:6] = fraction[:, 0, 0, :]
    packet[6:7] = jnp.where(lane < n, rows[0], 0.0)
    packet[7:8] = rows[1] * rows[1]
    mass[...] = rows[2]


SPREAD = -2.0 / math.log2(math.e)
FIRST = NB * (RX - 1)


def kernel(steps, bx, by, gz, n_x, n_y, *refs):
    (fraction, velocity, anchor, kinds, own_counts, table_hbm, target,
     vel_out, moved_out, pot,
     fraction_in, velocity_in, anchor_in, kinds_in, table, packet, mass, packets, wide, now, later, vel, moved,
     pk, pos, feat, hot, side_xy, side_type, near_xy, near_type, col_z, xy0, xy1, rates,
     acc, taps_x, taps_y, dens, dens_up, inv_ref, tgt_ref,
     send_sem, recv_sem, load_sem) = refs
    atoms = packet.shape[1]
    s, q = lax.axis_index("cells"), lax.axis_index("grp")
    rx, ry = bx + 5, by + 8
    near = [(-1, 0), (1, 0), (0, -1), (0, 1), (-1, -1), (1, 1), (-1, 1), (1, -1)]
    far = [(a, b) for a, b in NEIGHBOURS if abs(a) > 1]
    others = near + far

    barrier = pltpu.get_barrier_semaphore()
    total = jnp.int32(0)
    for a, b in NEIGHBOURS:
        there = exists(a, b)
        total = total + there.astype(jnp.int32)

        @pl.when(there)
        def _(a=a, b=b):
            pl.semaphore_signal(barrier, inc=1, device_id=(s + a, q + b), device_id_type=MESH)

    own_target = wide.at[6 : 6 + bx, 8 : 8 + by]
    loads = [
        pltpu.make_async_copy(src, dst, load_sem.at[k])
        for k, (src, dst) in enumerate(
            [(anchor, anchor_in), (fraction, fraction_in), (kinds, kinds_in), (table_hbm, table),
             (velocity, velocity_in), (target, own_target)]
        )
    ]
    for load in loads:
        load.start()
    for load in loads[:4]:
        load.wait()
    pack(fraction_in, anchor_in, kinds_in, own_counts, table, packet, mass)
    pl.semaphore_wait(barrier, total)

    def packet_copy(src, dst, group, a, b, there):
        mine, back = slot_of(a, b), slot_of(-a, -b)
        slot = back if there else mine
        return pltpu.make_async_remote_copy(
            src_ref=src,
            dst_ref=dst.at[slot],
            send_sem=send_sem.at[group, mine],
            recv_sem=recv_sem.at[group, slot],
            device_id=(s + a, q + b),
            device_id_type=MESH,
        )

    def target_copy(a, b, there):
        mine, back = slot_of(a, b), slot_of(-a, -b)
        slot = back if there else mine
        c, d = (-a, -b) if there else (a, b)
        x0, x1, y0, y1 = target_piece(c, d, bx, by)
        X, Y = 6 + c * bx + x0, 8 + d * by + y0
        return pltpu.make_async_remote_copy(
            src_ref=target.at[x0:x1, y0:y1],
            dst_ref=wide.at[X : X + x1 - x0, Y : Y + y1 - y0],
            send_sem=send_sem.at[1, mine],
            recv_sem=recv_sem.at[1, slot],
            device_id=(s + a, q + b),
            device_id_type=MESH,
        )

    def each(cells, act):
        for a, b in cells:

            @pl.when(exists(a, b))
            def _(a=a, b=b):
                act(a, b)

    each(others, lambda a, b: packet_copy(packet, packets, 0, a, b, True).start())
    for load in loads[4:]:
        load.wait()
    vel[...] = velocity_in[:, 0, 0, :]
    moved[...] = jnp.zeros_like(moved)

    row = lax.broadcasted_iota(jnp.int32, (8, atoms), 0)
    iz = iota_f((gz, atoms), 0).astype(BF16)

    def load_cell(step, a, b):
        slot = slot_of(a, b)
        own = isinstance(slot, int) and slot == OWN
        if step == 0:
            block = packet[...] if own else packets[slot]
            if not own:
                block = jnp.where(exists(a, b), block, 0.0)
            hot[slot] = jnp.where(
                iz == block[2:3].astype(BF16), jnp.ones((), BF16), jnp.zeros((), BF16)
            )
        else:
            block = pk[slot]
            fresh = now[...] if own else jnp.where(exists(a, b), later[slot], 0.0)
            block = jnp.concatenate([block[0:3], fresh, block[6:8]], 0)
        pk[slot] = block
        return slot, block

    def load_near(step, a, b):
        slot, block = load_cell(step, a, b)
        base_x = jnp.asarray(a * bx, F32)
        base_y = jnp.asarray(b * by, F32)
        base = jnp.where(row == 0, base_x, jnp.where(row == 1, base_y, 0.0))
        place = jnp.where(row < 3, block + pltpu.roll(block, 5, 0) + base, 0.0)
        pos[slot] = place
        feat[slot] = jnp.where(row == 3, 1.0, place) * block[6:7]
        h, m, l = split3(flat_of(place))
        near_xy[slot] = jnp.concatenate([h, m, h, l, h, m], 0)
        if step == 0:
            rate = 1.0 / (SPREAD * (type_width + block[7:8]))
            near_type[slot] = jnp.concatenate(split3(rate), 0)
        return slot

    def flat_of(place):
        x = place[0:1] - 0.5 * bx
        y = place[1:2] - 0.5 * by
        return jnp.where(
            row == 0, x, jnp.where(row == 1, y, jnp.where(row == 2, x * x + y * y, jnp.where(row == 3, 1.0, 0.0)))
        )

    types = table.shape[1]
    type_row = lax.broadcasted_iota(jnp.int32, (types, atoms), 0)
    type_width = jnp.zeros((types, atoms), F32)
    for t in range(types):
        type_width = jnp.where(type_row == t, table[1, t] * table[1, t], type_width)

    def own_side(step):
        p = flat_of(pos[OWN])
        turned = jnp.where(
            row < 2, -2.0 * p, jnp.where(row == 2, 1.0, jnp.where(row == 3, p[2:3], 0.0))
        )
        h, m, l = split3(turned)
        rows = jnp.concatenate([h, h, m, h, l, m], 0).astype(F32)
        side_xy[...] = jnp.transpose(rows).astype(BF16)
        col_z[...] = jnp.broadcast_to(jnp.transpose(pos[OWN])[:, 2:3], (atoms, 128))
        if step == 0:
            match = jnp.where(type_row == kinds_in[0], 1.0, 0.0)
            side_type[...] = jnp.transpose(jnp.concatenate([match] * 3, 0)).astype(BF16)

    def squares(step, slot, xy, rows=slice(None)):
        xy[rows] = dot_nn(side_xy[rows], near_xy[slot])
        if step == 0:
            rates[slot - FIRST, rows] = dot_nn(side_type[rows], near_type[slot])

    tall = min(16, atoms)

    def values(start, stop, *pairs):
        for r in range(start, stop, tall):
            rows = slice(r, r + tall)
            z = col_z[rows]
            sums = [acc[f, rows] for f in range(4)]
            for slot, xy in pairs:
                for k in range(0, atoms, 128):
                    at = slice(k, k + 128)
                    dz = z - pos[slot, 2:3, at]
                    rate = rates[slot - FIRST, rows, at]
                    value = jnp.exp2((xy[rows, at] + dz * dz) * rate) * rate
                    for f in range(4):
                        sums[f] = sums[f] + value * feat[slot, f : f + 1, at]
            for f in range(4):
                acc[f, rows] = sums[f]

    def spread(step, a, b):
        p0 = max(0, a * bx)
        p1 = min(rx, a * bx + bx + 5)
        r0, r1 = {-1: (0, 8), 0: (0, ry), 1: (by, ry)}[b]
        slot = slot_of(a, b)
        block = pk[slot]
        charge = block[6:7]
        ax, ay = block[0:1], block[1:2]
        fx, fy, fz = block[3:4], block[4:5], block[5:6]
        xs, ys = slice(0, p1 - p0), slice(0, r1 - r0)
        if step == 0:
            ax = ax + float(a * bx)
            ay = ay + float(b * by)
            in_x = ax + 1.0 + (s * bx).astype(F32) < float(n_x)
            in_y = ay + 1.0 + (q * by).astype(F32) < float(n_y)
            tx = iota_f((p1 - p0, atoms), 0) + float(p0 - 2) - ax
            ty = iota_f((r1 - r0, atoms), 0) + float(r0 - 2) - ay
            taps_x[slot, 0, xs] = tap_of(tx)
            taps_x[slot, 1, xs] = jnp.where(in_x, tap_of(tx - 1.0), 0.0)
            taps_y[slot, 0, ys] = tap_of(ty)
            taps_y[slot, 1, ys] = jnp.where(in_y, tap_of(ty - 1.0), 0.0)
        wx = taps_x[slot, 0, xs] * (1.0 - fx) + taps_x[slot, 1, xs] * fx
        wy = taps_y[slot, 0, ys] * (1.0 - fy) + taps_y[slot, 1, ys] * fy
        low, up = charge * (1.0 - fz), charge * fz
        planes = []
        for w in (wx * low, wx * up):
            plane = jnp.concatenate([wy * w[p : p + 1] for p in range(p1 - p0)], 0)
            planes.extend(split2(plane))
        size = planes[0].shape[0]
        out = dot_nt(jnp.concatenate(planes, 0), hot[slot])
        shape = (p1 - p0, r1 - r0, gz)
        dens[p0:p1, r0:r1] += (out[:size] + out[size : 2 * size]).reshape(shape)
        dens_up[p0:p1, r0:r1] += (out[2 * size : 3 * size] + out[3 * size :]).reshape(shape)

    i = lax.broadcasted_iota(jnp.int32, (gz, gz), 0)
    j = lax.broadcasted_iota(jnp.int32, (gz, gz), 1)
    blur_z = tap_of((i - j).astype(F32)).astype(BF16)
    blur_up = tap_of((i + 1 - j).astype(F32)).astype(BF16)

    def z_blur(x, matrix):
        h, l = split2(x)
        size = x.shape[0]
        both = dot_nn(jnp.concatenate([h, l], 0), matrix)
        return both[:size] + both[size:]

    gx = lax.broadcasted_iota(jnp.int32, (rx, ry, gz), 0) - 2 + s * bx
    gy = lax.broadcasted_iota(jnp.int32, (rx, ry, gz), 1) - 2 + q * by
    inside = (gx >= 0) & (gx < n_x) & (gy >= 0) & (gy < n_y)

    def scales():
        wxp, wyp = bx + 13, by + 16
        tx = lax.broadcasted_iota(jnp.int32, (wxp, wyp, gz), 0) - 6 + s * bx
        ty = lax.broadcasted_iota(jnp.int32, (wxp, wyp, gz), 1) - 8 + q * by
        valid = (tx >= 0) & (tx < n_x) & (ty >= 0) & (ty < n_y)
        t = jnp.where(valid, wide[...], 0.0)
        box_z = band(gz, 4, False)

        def boxed(v):
            two = v[:-1] + v[1:]
            four = two[:-2] + two[2:]
            eight = four[:-4] + four[4:]
            v = eight[:rx] + v[8 : 8 + rx]
            size = wyp
            two = v + pltpu.roll(v, size - 1, 1)
            four = two + pltpu.roll(two, size - 2, 1)
            eight = four + pltpu.roll(four, size - 4, 1)
            nine = eight + pltpu.roll(v, size - 8, 1)
            v = pltpu.roll(nine, size - 2, 1)[:, :ry]
            v = v.reshape(rx * ry, gz)
            h, m, l = split3(v)
            size = v.shape[0]
            out = dot_nn(jnp.concatenate([h, m, l], 0), box_z)
            out = out[:size] + out[size : 2 * size] + out[2 * size :]
            return out.reshape(rx, ry, gz) * (1.0 / 729.0)

        mean_one = boxed(t)
        mean_two = boxed(t * t)
        inverse_scale = lax.rsqrt(mean_two - mean_one * mean_one + EPSILON)
        inv_ref[...] = jnp.where(inside, inverse_scale, 0.0)
        tgt_ref[...] = pltpu.roll(t[4 : 4 + rx], wyp - 6, 1)[:, :ry]

    def map_part():
        size = rx * ry
        blurred = z_blur(dens[...].reshape(size, gz), blur_z)
        blurred = blurred + z_blur(dens_up[...].reshape(size, gz), blur_up)
        blurred = blurred.reshape(rx, ry, gz)
        residual = (blurred - tgt_ref[...]) * inv_ref[...]
        along = TAPS[0] * (residual[0 : bx + 1] + residual[4 : bx + 5])
        along = along + TAPS[1] * (residual[1 : bx + 2] + residual[3 : bx + 4])
        along = along + TAPS[2] * residual[2 : bx + 3]
        down = TAPS[0] * along
        for k in range(1, 5):
            down = down + TAPS[k] * pltpu.roll(along, ry - k, 1)
        return z_blur(down.reshape((bx + 1) * ry, gz), blur_z).reshape(bx + 1, ry, gz)

    def gradient_of(potential):
        px = lax.broadcasted_iota(jnp.int32, (bx + 1, ry, gz), 0) + s * bx
        py = lax.broadcasted_iota(jnp.int32, (bx + 1, ry, gz), 1) + q * by
        py_local = lax.broadcasted_iota(jnp.int32, (bx + 1, ry, gz), 1)
        field = jnp.where((px < n_x) & (py < n_y) & (py_local <= by), potential, 0.0)
        own = pk[OWN]
        ax, ay = own[0:1], own[1:2]
        fx, fy, fz = own[3:4], own[4:5], own[5:6]
        size = (bx + 1) * ry
        field = field.reshape(size, gz)
        up = pltpu.roll(field, gz - 1, 1)
        out = dot_nn(jnp.concatenate(split2(field) + split2(up), 0), hot[OWN])
        at_low = out[:size] + out[size : 2 * size]
        slope = out[2 * size : 3 * size] + out[3 * size :] - at_low
        value = at_low + fz * slope
        iy = iota_f((ry, atoms), 0)
        low_y = jnp.where(iy == ay, 1.0, 0.0)
        up_y = jnp.where(iy == ay + 1.0, 1.0, 0.0)
        wy = low_y * (1.0 - fy) + up_y * fy
        sy = up_y - low_y
        grad_x = jnp.zeros((1, atoms), F32)
        grad_y = jnp.zeros((1, atoms), F32)
        grad_z = jnp.zeros((1, atoms), F32)
        for p in range(bx + 1):
            low_x = jnp.where(ax == float(p), 1.0, 0.0)
            up_x = jnp.where(ax + 1.0 == float(p), 1.0, 0.0)
            wx = low_x * (1.0 - fx) + up_x * fx
            sx = up_x - low_x
            v = value[p * ry : (p + 1) * ry]
            g = slope[p * ry : (p + 1) * ry]
            grad_x = grad_x + sx * jnp.sum(wy * v, 0, keepdims=True)
            grad_y = grad_y + wx * jnp.sum(sy * v, 0, keepdims=True)
            grad_z = grad_z + wx * jnp.sum(wy * g, 0, keepdims=True)
        return own[6:7] * jnp.concatenate([grad_x, grad_y, grad_z], 0)

    for step in range(steps):
        last = step == steps - 1
        group = 0 if step == 0 else step + 1
        source, landing = (packet, packets) if step == 0 else (now, later)
        load_near(step, 0, 0)
        own_side(step)
        acc[...] = jnp.zeros_like(acc)
        dens[...] = jnp.zeros_like(dens)
        dens_up[...] = jnp.zeros_like(dens_up)
        squares(step, OWN, xy0)
        values(0, atoms, (OWN, xy0))
        spread(step, 0, 0)

        def two_cells(k, carry):
            da = jnp.where(k == 1, 0, 1)
            db = jnp.where(k == 0, 0, jnp.where(k == 3, -1, 1))
            each([(-da, -db), (da, db)], lambda a, b: packet_copy(source, landing, group, a, b, False).wait_recv())

            if step == 0:

                @pl.when(k == 0)
                def _():
                    each(others, lambda a, b: target_copy(a, b, True).start())

            one = load_near(step, -da, -db)
            two = load_near(step, da, db)
            for h in range(0, atoms, 64):
                part = slice(h, h + 64)
                squares(step, one, xy0, part)
                squares(step, two, xy1, part)
                if h > 0:
                    values(h - 64, h, (one, xy0), (two, xy1))
            values(atoms - 64, atoms, (one, xy0), (two, xy1))
            return carry

        lax.fori_loop(0, len(near) // 2, two_cells, 0)
        each(far, lambda a, b: packet_copy(source, landing, group, a, b, False).wait_recv())
        for a, b in far:
            load_cell(step, a, b)
        for a, b in others:
            spread(step, a, b)
        if step == 0:
            each(others, lambda a, b: target_copy(a, b, False).wait_recv())
            scales()
        potential = map_part()
        if last:
            pot[...] = potential[:bx, :by]
        gradient = gradient_of(potential)
        lane = lax.broadcasted_iota(jnp.int32, (atoms, 128), 1)
        turned = jnp.zeros((atoms, 128), F32)
        for f in range(4):
            turned = jnp.where(lane == f, jnp.sum(acc[f], 1, keepdims=True), turned)
        sums = jnp.transpose(turned)[0:8]
        here = pos[OWN][0:3]
        pair = (SPREAD * pk[OWN][6:7]) * (here * sums[3:4] - sums[0:3])
        new_velocity = vel[...] + TIME_STEP * (pair - gradient) / mass[...]
        new_moved = moved[...] + TIME_STEP * new_velocity
        if last:
            vel_out[...] = new_velocity
            moved_out[...] = new_moved
        else:
            vel[...] = new_velocity
            moved[...] = new_moved
            now[...] = pk[OWN][3:6] + TIME_STEP * new_velocity
            each(others, lambda a, b: packet_copy(now, later, step + 2, a, b, True).start())

    each(others, lambda a, b: packet_copy(packet, packets, 0, a, b, True).wait_send())
    each(others, lambda a, b: target_copy(a, b, True).wait_send())
    for step in range(1, steps):
        each(others, lambda a, b: packet_copy(now, later, step + 1, a, b, True).wait_send())


STEPS = 2


def finish(counts, vel, moved, pot, vel_out, moved_out, pot_out):
    live = lax.broadcasted_iota(jnp.int32, vel.shape, 1) < counts[0, 0]
    vel_out[:, 0, 0, :] = jnp.where(live, vel[...], 0.0)
    moved_out[:, 0, 0, :] = jnp.where(live, moved[...], 0.0)
    pot_out[...] = pot[...]


def in_hbm(x):
    return pltpu.with_memory_space_constraint(x, pltpu.HBM)


def per_device(fraction, velocity, anchor, atom_types, counts, type_table, target):
    atoms = fraction.shape[3]
    bx, by, gz = target.shape
    types = type_table.shape[1]
    n_x = bx * lax.axis_size("cells")
    n_y = by * lax.axis_size("grp")
    row = jax.ShapeDtypeStruct((3, atoms), F32)
    final = jax.ShapeDtypeStruct(velocity.shape, F32)
    field = jax.ShapeDtypeStruct((bx, by, gz), F32)
    region = pltpu.VMEM((bx + 5, by + 8, gz), F32)
    three = pltpu.VMEM((3, atoms), F32)
    square = pltpu.VMEM((atoms, atoms), F32)
    done = pl.pallas_call(
        functools.partial(kernel, STEPS, bx, by, gz, n_x, n_y),
        out_shape=[row, row, field],
        in_specs=[HBM, HBM, HBM, HBM, SMEM, HBM, HBM],
        out_specs=[VMEM] * 3,
        scratch_shapes=[
            pltpu.VMEM(fraction.shape, F32),
            pltpu.VMEM(velocity.shape, F32),
            pltpu.VMEM(anchor.shape, jnp.int32),
            pltpu.VMEM(atom_types.shape, jnp.int32),
            pltpu.SMEM(type_table.shape, F32),
            pltpu.VMEM((8, atoms), F32),
            pltpu.VMEM((1, atoms), F32),
            pltpu.VMEM((SLOTS, 8, atoms), F32),
            pltpu.VMEM((bx + 13, by + 16, gz), F32),
            three,
            pltpu.VMEM((SLOTS, 3, atoms), F32),
            three,
            three,
            pltpu.VMEM((SLOTS, 8, atoms), F32),
            pltpu.VMEM((SLOTS, 8, atoms), F32),
            pltpu.VMEM((SLOTS, 8, atoms), F32),
            pltpu.VMEM((SLOTS, gz, atoms), BF16),
            pltpu.VMEM((atoms, 48), BF16),
            pltpu.VMEM((atoms, 3 * types), BF16),
            pltpu.VMEM((SLOTS, 48, atoms), BF16),
            pltpu.VMEM((SLOTS, 3 * types, atoms), BF16),
            pltpu.VMEM((atoms, 128), F32),
            square,
            square,
            pltpu.VMEM((3 * NB, atoms, atoms), F32),
            pltpu.VMEM((4, atoms, 128), F32),
            pltpu.VMEM((SLOTS, 2, bx + 5, atoms), F32),
            pltpu.VMEM((SLOTS, 2, by + 8, atoms), F32),
            region,
            region,
            region,
            region,
            pltpu.SemaphoreType.DMA((STEPS + 1, SLOTS)),
            pltpu.SemaphoreType.DMA((STEPS + 1, SLOTS)),
            pltpu.SemaphoreType.DMA((6,)),
        ],
        compiler_params=pltpu.CompilerParams(
            collective_id=0, has_side_effects=True, vmem_limit_bytes=40 * 2**20
        ),
        name="dynamics",
    )(*map(in_hbm, (fraction, velocity, anchor, atom_types)), counts, in_hbm(type_table), in_hbm(target))
    return tuple(
        pl.pallas_call(
            finish,
            out_shape=[final, final, field],
            in_specs=[SMEM, VMEM, VMEM, VMEM],
            out_specs=[VMEM] * 3,
            compiler_params=pltpu.CompilerParams(vmem_limit_bytes=4 * 2**20),
            name="finish",
        )(counts, *done)
    )


def solution(mesh):
    placed = (
        P(None, "cells", "grp", None),
        P(None, "cells", "grp", None),
        P(None, "cells", "grp", None),
        P("cells", "grp", None),
        P("cells", "grp"),
        P(),
        P("cells", "grp", None),
    )
    return jax.shard_map(
        per_device,
        mesh=mesh,
        in_specs=placed,
        out_specs=(
            P(None, "cells", "grp", None),
            P(None, "cells", "grp", None),
            P("cells", "grp", None),
        ),
        check_vma=False,
    )
```
